128 devices in a mesh: level: 16 (over y_lo, z, core), member: 8 (over y_hi, x).
Axes of the slice: x: 4, y: 4 (y_hi: 2, y_lo: 2; y = y_hi * 2 + y_lo), z: 4, core: 2. Of those that a mesh axis runs over, the one named last changes fastest.
Arguments:
- model_state: float32 [8, 32, 4, 256, 512], P('member', 'level'), may hold values from -6 to 6
- noise_field: bfloat16 [8, 32, 4, 256, 512], P('member', 'level'), may hold values from -5 to 5
- cotangent: bfloat16 [8, 32, 4, 256, 512], P('member', 'level'), may hold values from -6 to 6
- zonal_shift: float32 [32, 4], P('level'), may hold values from -0.02 to 0.02
- viscosity: float32 [32, 4], P('level'), may hold values from 0.1 to 3
- noise_scale: float32 [32, 4], P('level'), may hold values from 0.2 to 1
- w_in: bfloat16 [128, 384], replicated, may hold values from -0.5 to 0.5
- b_in: float32 [384], replicated, may hold values from -3 to 3
- w_mid: bfloat16 [384, 384], replicated, may hold values from -0.3125 to 0.3125
- b_mid: float32 [384], replicated, may hold values from -3 to 3
- w_out: bfloat16 [384, 128], replicated, may hold values from -0.3125 to 0.3125
Outputs:
- next_state: float32 [8, 32, 4, 256, 512], P('member', 'level')
- state_grad: float32 [8, 32, 4, 256, 512], P('member', 'level')
- grad_w_in: float32 [128, 384], P(None, ('level', 'member'))
- grad_w_mid: float32 [384, 384], P(None, ('level', 'member'))
- grad_w_out: float32 [128, 384], P(None, ('level', 'member'))
- grad_bias: float32 [2, 384], P(None, ('level', 'member'))
The draws below stay inside these ranges and needn't reach their ends.
All inputs are finite; a program needn't handle non-finite values.
Results may differ from the reference program's by a relative error of at most 0.0085.
Values may be sent and summed in bfloat16 or wider, within the bound.
A program may use at most 128 MiB of HBM per device.

```python
import math
import jax
import jax.numpy as jnp
from jax import lax

L = 32
F = 4
NLAT = 256
NLON = 512
WAVES = 128
MODES = 128
H = 384
MEMBERS = 8
HIN = 128
HOUT = 128


def levels(own_key, extent, shards, low, top_value):
    def one(axis_at, parts):
        heights = jax.random.uniform(jax.random.fold_in(jax.random.fold_in(own_key, 6), axis_at), (parts,), jnp.float32, low / len(shards), top_value / len(shards))
        return jnp.repeat(jnp.exp(heights), extent[axis_at] // parts).reshape((-1,) + (1,) * (len(extent) - axis_at - 1))

    gain = one(*shards[0])
    for cut in shards[1:]:
        gain = gain * one(*cut)
    return gain


def normal_values(own_key, shape, spread, reach, cuts=(), kind=jnp.bfloat16):
    loudness = levels(own_key, shape, cuts, -0.22, 0.18) if cuts else 1.0
    result = jax.random.normal(own_key, shape, jnp.float32) * spread * loudness
    return jnp.minimum(jnp.maximum(result, -reach), reach).astype(kind)


def setup_inputs(seed: int = 0) -> dict:
    key_list = jax.random.split(jax.random.key(seed), 12)
    return {
        "model_state": normal_values(key_list[0], (MEMBERS, L, F, NLAT, NLON), 1.0, 6.0, ((0, 8), (1, 16)), jnp.float32),
        "noise_field": normal_values(key_list[1], (MEMBERS, L, F, NLAT, NLON), 1.0, 5.0, ((0, 8), (1, 16))),
        "cotangent": normal_values(key_list[2], (MEMBERS, L, F, NLAT, NLON), 1.0, 6.0, ((0, 8), (1, 16))),
        "zonal_shift": jnp.clip(jax.random.uniform(key_list[3], (L, F), jnp.float32, -0.02, 0.02) * levels(key_list[3], (L, F), ((0, 16),), -0.4, 0.0), -0.02, 0.02),
        "viscosity": jnp.clip(jnp.exp(math.log(3.0) - 3.4011974 * jax.random.uniform(key_list[4], (L, F), jnp.float32) ** levels(key_list[4], (L, F), ((0, 16),), -0.2, 0.2)), 0.1, 3.0),
        "noise_scale": jnp.clip(0.2 + 0.8 * jax.random.uniform(key_list[5], (L, F), jnp.float32) ** levels(key_list[5], (L, F), ((0, 16),), -0.2, 0.2), 0.2, 1.0),
        "w_in": normal_values(key_list[6], (HIN, H), HIN ** -0.5, 0.5),
        "b_in": normal_values(key_list[7], (H,), 0.5, 3.0, (), jnp.float32),
        "w_mid": normal_values(key_list[8], (H, H), H ** -0.5, 0.3125),
        "b_mid": normal_values(key_list[9], (H,), 0.5, 3.0, (), jnp.float32),
        "w_out": normal_values(key_list[10], (H, HOUT), H ** -0.5, 0.3125),
    }


def spectral_tables(lat_count, lon_count):
    lon_index = jnp.arange(lon_count, dtype=jnp.float32)
    wave_index = jnp.arange(WAVES, dtype=jnp.float32)
    phases = 2.0 * jnp.pi * lon_index[:, None] * wave_index[None, :] / lon_count
    lon_fwd = jnp.concatenate([jnp.cos(phases), jnp.sin(phases)], axis=1)
    wave_weight = jnp.where(wave_index == 0, 1.0, 2.0) / lon_count
    lon_inv = lon_fwd * jnp.concatenate([wave_weight, wave_weight])[None, :]
    lat_index = jnp.arange(lat_count, dtype=jnp.float32)
    mode_index = jnp.arange(MODES, dtype=jnp.float32)
    lat_fwd = jnp.cos(jnp.pi * (lat_index[:, None] + 0.5) * mode_index[None, :] / lat_count)
    lat_inv = lat_fwd * (jnp.where(mode_index == 0, 1.0, 2.0) / lat_count)[None, :]
    return (lon_fwd, lon_inv, lat_fwd, lat_inv)

def spectral_step(fields, zonal_shift, viscosity):
    lon_fwd, lon_inv, lat_fwd, lat_inv = spectral_tables(fields.shape[3], fields.shape[4])
    highest = lax.Precision.HIGHEST
    partial_lon = jnp.einsum('mlfij,jk->mlfik', fields, lon_fwd, precision=highest)
    spectrum = jnp.einsum('mlfik,ip->mlfpk', partial_lon, lat_fwd, precision=highest)
    wave_index = jnp.arange(WAVES, dtype=jnp.float32)
    mode_index = jnp.arange(MODES, dtype=jnp.float32)
    radial = (wave_index / WAVES)[None, :] ** 2 + (mode_index / MODES)[:, None] ** 2
    damping = jnp.exp(-viscosity[:, :, None, None] * radial[None, None])
    phases = zonal_shift[:, :, None, None] * wave_index[None, None, None, :]
    cosine = jnp.cos(phases) * damping
    sine = jnp.sin(phases) * damping
    cos_part = spectrum[..., :WAVES]
    sin_part = spectrum[..., WAVES:]
    rotated = jnp.concatenate([cos_part * cosine - sin_part * sine, cos_part * sine + sin_part * cosine], axis=-1)
    halfway = jnp.einsum('mlfpk,ip->mlfik', rotated, lat_inv, precision=highest)
    return jnp.einsum('mlfik,jk->mlfij', halfway, lon_inv, precision=highest)

def silu_slope(values):
    sigmoid = jax.nn.sigmoid(values)
    return sigmoid * (1.0 + values * (1.0 - sigmoid))

def reference(model_state, noise_field, cotangent, zonal_shift, viscosity, noise_scale, w_in, b_in, w_mid, b_mid, w_out):
    hidden = w_in.shape[1]
    inputs_count = w_in.shape[0]
    norm_scale = 1.0 / math.sqrt(MEMBERS * NLAT * NLON)

    def member_step(carry, members_in):
        state_one, noise_one, cotan_one = members_in
        dynamics = spectral_step(state_one[None], zonal_shift, viscosity)[0]
        level_shape = dynamics.shape
        inputs_bf = dynamics.astype(jnp.bfloat16).reshape(inputs_count, -1)
        pre_one = jnp.dot(w_in.T, inputs_bf, preferred_element_type=jnp.float32) + b_in[:, None]
        act_one = jax.nn.silu(pre_one).astype(jnp.bfloat16)
        pre_two = jnp.dot(w_mid.T, act_one, preferred_element_type=jnp.float32) + b_mid[:, None]
        act_two = jax.nn.silu(pre_two).astype(jnp.bfloat16)
        tendency = jnp.dot(w_out.T, act_two, preferred_element_type=jnp.float32).astype(jnp.bfloat16)
        factor = 1.0 + noise_scale[:, :, None, None] * noise_one.astype(jnp.float32)
        next_one = dynamics + tendency.astype(jnp.float32).reshape(level_shape) * factor
        grad_tend = (cotan_one.astype(jnp.float32) * factor).astype(jnp.bfloat16).reshape(inputs_count, -1)
        gw_out = jnp.dot(grad_tend, act_two.T, preferred_element_type=jnp.float32)
        slope_two = (jnp.dot(w_out, grad_tend, preferred_element_type=jnp.float32) * silu_slope(pre_two)).astype(jnp.bfloat16)
        gw_mid = jnp.dot(act_one, slope_two.T, preferred_element_type=jnp.float32)
        slope_one = (jnp.dot(w_mid, slope_two, preferred_element_type=jnp.float32) * silu_slope(pre_one)).astype(jnp.bfloat16)
        gw_in = jnp.dot(inputs_bf, slope_one.T, preferred_element_type=jnp.float32)
        gbias = jnp.stack([lax.optimization_barrier(jnp.sum(slope_one.astype(jnp.float32), axis=1)), lax.optimization_barrier(jnp.sum(slope_two.astype(jnp.float32), axis=1))])
        back_inputs = jnp.dot(w_in, slope_one, preferred_element_type=jnp.float32).astype(jnp.bfloat16)
        grad_levels = cotan_one.astype(jnp.float32) + back_inputs.astype(jnp.float32).reshape(level_shape)
        unused, pullback = jax.vjp(lambda fields: spectral_step(fields, zonal_shift, viscosity), state_one[None])
        grad_one = pullback(grad_levels[None])[0][0]
        carry = (carry[0] + gw_in, carry[1] + gw_mid, carry[2] + gw_out, carry[3] + gbias)
        return (carry, (next_one, grad_one))
    start = (jnp.zeros((inputs_count, hidden), jnp.float32), jnp.zeros((hidden, hidden), jnp.float32), jnp.zeros((w_out.shape[1], hidden), jnp.float32), jnp.zeros((2, hidden), jnp.float32))
    sums, outputs = lax.scan(member_step, start, (model_state, noise_field, cotangent))
    next_state, state_grad = outputs
    return (next_state, state_grad, sums[0] * norm_scale, sums[1] * norm_scale, sums[2] * norm_scale, sums[3] * norm_scale)
```

```python
import functools
import math

import jax
import jax.numpy as jnp
import ml_dtypes
import numpy as np
from jax import lax
from jax.experimental import pallas as pl
from jax.experimental.pallas import tpu as pltpu
from jax.sharding import PartitionSpec as P

WAVES = 128
MODES = 128
F32 = jnp.float32
BF16 = jnp.bfloat16
MESH = pl.DeviceIdType.MESH


def halves_np(table):
    high = table.astype(ml_dtypes.bfloat16)
    low = (table - high.astype(np.float64)).astype(ml_dtypes.bfloat16)
    return high, low


def tables(lat_count, lon_count):
    lon = np.arange(lon_count)[:, None] * np.arange(WAVES)[None, :] % lon_count
    phase = 2.0 * np.pi * lon / lon_count
    lon_fwd = np.concatenate([np.cos(phase), np.sin(phase)], axis=1)
    turn = (2 * np.arange(lat_count)[:, None] + 1) * np.arange(MODES)[None, :] % (4 * lat_count)
    lat_fwd = np.cos(np.pi * turn / (2 * lat_count))
    out = []
    for table in (lon_fwd, lon_fwd.T, lat_fwd, lat_fwd.T):
        out.extend(halves_np(np.ascontiguousarray(table)))
    return out


def halves(x):
    high = x.astype(BF16)
    return high, (x - high.astype(F32)).astype(BF16)


def dot(a, b):
    return jnp.dot(a, b, preferred_element_type=F32)


def dot_nt(a, b):
    return lax.dot_general(a, b, (((1,), (1,)), ((), ())), preferred_element_type=F32)


def dot3(a, b):
    return dot(a[0], b[0]) + dot(a[0], b[1]) + dot(a[1], b[0])


def put_rows(ref, rows, x):
    for c in range(x.shape[1] // 128):
        ref[c, rows, :] = x[:, c * 128 : (c + 1) * 128]


def get_rows(ref, rows, first, count):
    return jnp.concatenate([ref[c, rows, :] for c in range(first, first + count)], axis=1)


def sigmoid(x):
    return 0.5 * jnp.tanh(0.5 * x) + 0.5


def kernel(
    levels, members, lat_count, lon_count, hidden,
    shift_ref, visc_ref, ns_ref, state_hbm, noise_hbm, cot_hbm,
    w_in_ref, b_in_ref, w_mid_ref, b_mid_ref, w_out_ref,
    lfh_ref, lfl_ref, lth_ref, ltl_ref, lah_ref, lal_ref, ath_ref, atl_ref,
    next_hbm, grad_hbm, gin_ref, gmid_ref, gout_ref, gbias_ref,
    state_v, noise_v, cot_v, g16, rg, h16, rh, tb, tbr, next_v, z_v, h32, st_v, t_v,
    win_t, wmid_t, wout_t, bb1, bb2, cs_v, sn_v, gi_a, gm_a, go_a, s1_a, s2_a,
    gs, gr, ms, mr,
    in_sem, out_sem, g_send, g_recv, h_send, h_recv, t_send, t_recv, s_send, s_recv, m_send, m_recv,
):
    me = lax.axis_index("level")
    mem = lax.axis_index("member")
    blocks = lat_count // 32
    fields = 8
    waves = 2 * WAVES
    lon_tiles = lon_count // 128
    wave_tiles = waves // 128

    load_noise = pltpu.make_async_copy(noise_hbm, noise_v, in_sem.at[0])
    load_cot = pltpu.make_async_copy(cot_hbm, cot_v, in_sem.at[1])
    load_state = pltpu.make_async_copy(state_hbm, state_v, in_sem.at[2])
    load_noise.start()
    load_cot.start()
    load_state.start()

    barrier = pltpu.get_barrier_semaphore()

    def greet_level(d, _):
        pl.semaphore_signal(
            barrier, inc=1, device_id={"level": lax.rem(me + d, levels)}, device_id_type=MESH
        )
        return 0

    def greet_member(d, _):
        pl.semaphore_signal(
            barrier, inc=1, device_id={"member": lax.rem(mem + d, members)}, device_id_type=MESH
        )
        return 0

    lax.fori_loop(1, levels, greet_level, 0)
    lax.fori_loop(1, members, greet_member, 0)
    pl.semaphore_wait(barrier, levels + members - 2)

    def noise_scale(f):
        return ns_ref[f // 4, f % 4]

    load_noise.wait()
    load_cot.wait()

    def make_grad(a, _):
        rows = pl.ds(pl.multiple_of(a * 32, 32), 32)
        for f in range(fields):
            factor = 1.0 + noise_scale(f) * noise_v[f, rows, :].astype(F32)
            put_rows(st_v, pl.ds(f, 32, stride=fields), cot_v[f, rows, :].astype(F32) * factor)
        g16[a] = get_rows(st_v, slice(None), 0, lon_tiles).astype(BF16).reshape(levels, 16, lon_count)
        return 0

    lax.fori_loop(0, blocks, make_grad, 0)

    def send_grad(d, _):
        to = lax.rem(me + d, levels)
        pltpu.make_async_remote_copy(
            g16.at[:, pl.ds(to, 1)], rg.at[:, pl.ds(me, 1)], g_send, g_recv,
            device_id={"level": to}, device_id_type=MESH,
        ).start()
        return 0

    lax.fori_loop(1, levels, send_grad, 0)
    rg[:, pl.ds(me, 1)] = g16[:, pl.ds(me, 1)]

    field_row = lax.broadcasted_iota(jnp.int32, (fields, WAVES), 0)
    wave = lax.broadcasted_iota(jnp.int32, (fields, WAVES), 1).astype(F32)
    shift = jnp.zeros((fields, WAVES), F32)
    for f in range(fields):
        shift = jnp.where(field_row == f, shift_ref[f // 4, f % 4], shift)
    cs_v[...] = jnp.cos(shift * wave)
    sn_v[...] = jnp.sin(shift * wave)
    p_index = lax.broadcasted_iota(jnp.int32, (MODES, WAVES), 0).astype(F32)
    k_index = lax.broadcasted_iota(jnp.int32, (MODES, WAVES), 1).astype(F32)
    radial = (k_index / WAVES) ** 2 + (p_index / MODES) ** 2
    weight = (
        jnp.where(p_index == 0, 1.0, 2.0) / lat_count * (jnp.where(k_index == 0, 1.0, 2.0) / lon_count)
    )

    def rotation(f):
        damping = jnp.exp(-visc_ref[f // 4, f % 4] * radial) * weight
        return cs_v[pl.ds(f, 1), :] * damping, sn_v[pl.ds(f, 1), :] * damping

    lf = (lfh_ref, lfl_ref)
    lt = (lth_ref, ltl_ref)
    la = (lah_ref, lal_ref)
    at = (ath_ref, atl_ref)

    def both(pair):
        return pair[0][...], pair[1][...]

    load_state.wait()

    def forward(f, _):
        partial = halves(dot3(halves(state_v[f]), both(lf)))
        spectrum = dot3(both(at), partial)
        cosine, sine = rotation(f)
        a, b = spectrum[:, :WAVES], spectrum[:, WAVES:]
        rotated = jnp.concatenate([a * cosine - b * sine, a * sine + b * cosine], axis=1)
        put_rows(h32, pl.ds(f, lat_count, stride=fields), dot3(both(la), halves(rotated)))
        return 0

    lax.fori_loop(0, fields, forward, 0)

    def pack_rows(a, _):
        rows = pl.ds(pl.multiple_of(a * 256, 256), 256)
        h16[a] = get_rows(h32, rows, 0, wave_tiles).astype(BF16).reshape(levels, 16, waves)
        return 0

    lax.fori_loop(0, blocks, pack_rows, 0)

    def send_rows(d, _):
        to = lax.rem(me + d, levels)
        pltpu.make_async_remote_copy(
            h16.at[:, pl.ds(to, 1)], rh.at[:, pl.ds(me, 1)], h_send, h_recv,
            device_id={"level": to}, device_id_type=MESH,
        ).start()
        return 0

    lax.fori_loop(1, levels, send_rows, 0)
    rh[:, pl.ds(me, 1)] = h16[:, pl.ds(me, 1)]

    win_t[...] = w_in_ref[...].astype(F32).T.astype(BF16)
    wmid_t[...] = w_mid_ref[...].astype(F32).T.astype(BF16)
    wout_t[...] = w_out_ref[...].astype(F32).T.astype(BF16)
    bb1[...] = jnp.broadcast_to(b_in_ref[...], (128, hidden)).T
    bb2[...] = jnp.broadcast_to(b_mid_ref[...], (128, hidden)).T
    gi_a[...] = jnp.zeros_like(gi_a)
    gm_a[...] = jnp.zeros_like(gm_a)
    go_a[...] = jnp.zeros_like(go_a)
    s1_a[...] = jnp.zeros_like(s1_a)
    s2_a[...] = jnp.zeros_like(s2_a)

    def local(f, _):
        rows = get_rows(h32, pl.ds(f, lat_count, stride=fields), 0, wave_tiles)
        next_v[f] = dot3(halves(rows), both(lt))
        cot = cot_v[f]
        z_v[f] = dot(cot, lfh_ref[...]) + dot(cot, lfl_ref[...])
        return 0

    lax.fori_loop(0, fields, local, 0)

    others = pl.ds(0, levels - 1)

    def wait_for(ref, sem):
        pltpu.make_async_copy(ref, ref, sem).wait()

    wait_for(rg.at[:, others], g_recv)
    wait_for(rh.at[:, others], h_recv)

    def lanes(x):
        x = x.reshape(levels, 2, 8, lon_count)
        return jnp.concatenate(
            [x[:, r].reshape(levels * 8, lon_count) for r in range(2)], axis=1
        ).astype(BF16)

    def rows_of(x0, x1, width):
        parts = [x.reshape(levels, 8, width) for x in (x0, x1)]
        return jnp.concatenate(parts, axis=1).astype(BF16)

    def lane_sum(x):
        out = x[:, :128]
        for c in range(1, x.shape[1] // 128):
            out = out + x[:, c * 128 : (c + 1) * 128]
        return out

    cols = 2 * lon_count

    def columns(a, _):
        spec = rh[a].reshape(levels * 16, waves)
        inp = lanes(dot(spec, lth_ref[...]) + dot(spec, ltl_ref[...]))
        gt = lanes(rg[a].reshape(levels * 16, lon_count).astype(F32))
        pre = dot(win_t[...], inp) + jnp.tile(bb1[...], (1, cols // 128))
        sg = sigmoid(pre)
        act = pre * sg
        slope1 = sg + act * (1.0 - sg)
        act1 = act.astype(BF16)
        pre = dot(wmid_t[...], act1) + jnp.tile(bb2[...], (1, cols // 128))
        sg = sigmoid(pre)
        act = pre * sg
        slope2 = sg + act * (1.0 - sg)
        act2 = act.astype(BF16)
        tend = dot(wout_t[...], act2)
        tb[a, :, :, pl.ds(0, lon_count)] = rows_of(tend[:, :lon_count], tend[:, lon_count:], lon_count)
        go_a[...] += dot_nt(act2, gt)
        slope = dot(w_out_ref[...], gt) * slope2
        s2_a[...] += lane_sum(slope)
        s2 = slope.astype(BF16)
        gm_a[...] += dot_nt(s2, act1)
        slope = dot(w_mid_ref[...], s2) * slope1
        s1_a[...] += lane_sum(slope)
        s1 = slope.astype(BF16)
        gi_a[...] += dot_nt(s1, inp)
        back = dot(w_in_ref[...], s1).astype(BF16)
        back = jnp.concatenate([back[:, :lon_count], back[:, lon_count:]], axis=0)
        back = dot(back, lfh_ref[...]) + dot(back, lfl_ref[...])
        half = levels * 8
        tb[a, :, :, pl.ds(lon_count, waves)] = rows_of(back[:half], back[half:], waves)

        def send_back(d, _):
            to = lax.rem(me + d, levels)
            pltpu.make_async_remote_copy(
                tb.at[a, pl.ds(to, 1)], tbr.at[a, pl.ds(me, 1)], t_send, t_recv.at[a],
                device_id={"level": to}, device_id_type=MESH,
            ).start()
            return 0

        lax.fori_loop(1, levels, send_back, 0)
        tbr[a, pl.ds(me, 1)] = tb[a, pl.ds(me, 1)]
        return 0

    lax.fori_loop(0, blocks, columns, 0)

    share = hidden // levels
    groups = share // 8
    width = 640

    def column_sum(x):
        return jnp.sum(x, axis=1, keepdims=True)

    lane = lax.broadcasted_iota(jnp.int32, (8, 128), 1)

    def pack_grads(t, _):
        start = t * share
        pieces = []
        bias = jnp.zeros((8, 128), F32)
        for g in range(groups):
            rows = pl.ds(pl.multiple_of(start + 8 * g, 8), 8)
            pieces.append(jnp.concatenate([gi_a[rows, :], gm_a[rows, :], go_a[rows, :]], axis=1))
            bias = jnp.where(lane == 2 * g, column_sum(s1_a[rows, :]), bias)
            bias = jnp.where(lane == 2 * g + 1, column_sum(s2_a[rows, :]), bias)
        top = jnp.concatenate([pieces[0], pieces[2][:, :384]], axis=1)
        low = jnp.concatenate([pieces[1], pieces[2][:, 384:], bias], axis=1)
        gs[t] = jnp.concatenate([top, low], axis=0).astype(BF16)
        return 0

    lax.fori_loop(0, levels, pack_grads, 0)

    def send_grads(d, _):
        to = lax.rem(me + d, levels)
        pltpu.make_async_remote_copy(
            gs.at[pl.ds(to, 1)], gr.at[pl.ds(me, 1)], s_send, s_recv,
            device_id={"level": to}, device_id_type=MESH,
        ).start()
        return 0

    lax.fori_loop(1, levels, send_grads, 0)
    gr[pl.ds(me, 1)] = gs[pl.ds(me, 1)]

    def arrive(a, _):
        wait_for(tbr.at[a, others], t_recv.at[a])
        put_rows(t_v, slice(None), tbr[a].astype(F32).reshape(256, lon_count + waves))
        rows = pl.ds(pl.multiple_of(a * 32, 32), 32)
        for f in range(fields):
            mine = pl.ds(f, 32, stride=fields)
            factor = 1.0 + noise_scale(f) * noise_v[f, rows, :].astype(F32)
            next_v[f, rows, :] += get_rows(t_v, mine, 0, lon_tiles) * factor
            z_v[f, rows, :] += get_rows(t_v, mine, lon_tiles, wave_tiles)
        pltpu.make_async_copy(next_v.at[:, rows], next_hbm.at[:, rows], out_sem.at[0]).start()
        return 0

    lax.fori_loop(0, blocks - 1, arrive, 0)

    wait_for(gr.at[others], s_recv)
    total = gr[0].astype(F32)
    for s in range(1, levels):
        total = total + gr[s].astype(F32)
    ms[...] = total.astype(BF16)

    def send_sums(d, _):
        to = lax.rem(mem + d, members)
        pltpu.make_async_remote_copy(
            ms, mr.at[mem], m_send, m_recv, device_id={"member": to}, device_id_type=MESH
        ).start()
        return 0

    lax.fori_loop(1, members, send_sums, 0)
    mr[mem] = ms[...]

    arrive(blocks - 1, 0)

    def backward(f, _):
        spectrum = dot3(both(at), halves(z_v[f]))
        cosine, sine = rotation(f)
        a, b = spectrum[:, :WAVES], spectrum[:, WAVES:]
        turned = jnp.concatenate([a * cosine + b * sine, b * cosine - a * sine], axis=1)
        rows = halves(dot3(both(la), halves(turned)))
        state_v[f] = dot3(rows, both(lt))
        pltpu.make_async_copy(state_v.at[f], grad_hbm.at[f], out_sem.at[1]).start()
        return 0

    lax.fori_loop(0, fields, backward, 0)

    wait_for(mr.at[pl.ds(0, members - 1)], m_recv)
    total = mr[0].astype(F32)
    for s in range(1, members):
        total = total + mr[s].astype(F32)
    total = total * (1.0 / math.sqrt(members * lat_count * lon_count))
    third = jnp.concatenate([total[:8, width:], total[8:, width : width + 256]], axis=1)
    bias = total[8:, width + 256 :]
    own = share // members
    picked = jnp.concatenate([total[:8, :width], total[8:, :width], third], axis=0)
    unit = lax.broadcasted_iota(jnp.int32, (share, 128), 0)
    slot = lax.broadcasted_iota(jnp.int32, (share, 128), 1)
    choose = jnp.where((unit == mem * own + slot) & (slot < own), 1.0, 0.0)

    def select(block, pick):
        return lax.dot_general(
            block, pick, (((0,), (0,)), ((), ())),
            precision=lax.Precision.HIGHEST, preferred_element_type=F32,
        )

    gin_ref[...] = select(picked[:, :128], choose)[:, :own]
    gmid_ref[...] = select(picked[:, 128:512], choose)[:, :own]
    gout_ref[...] = select(picked[:, 512:640], choose)[:, :own]
    sums = jnp.zeros((128, 128), F32)
    for g in range(groups):
        part = select(bias, choose[8 * g : 8 * g + 8])
        sums = sums + jnp.concatenate([part[2 * g : 2 * g + 2], jnp.zeros((126, 128), F32)], axis=0)
    gbias_ref[...] = sums[:2, :own]

    wait_for(g16.at[:, others], g_send)
    wait_for(h16.at[:, others], h_send)
    wait_for(tb.at[:, others], t_send)
    wait_for(gs.at[others], s_send)
    wait_for(mr.at[pl.ds(0, members - 1)], m_send)
    pltpu.make_async_copy(next_v, next_hbm, out_sem.at[0]).wait()
    pltpu.make_async_copy(state_v, grad_hbm, out_sem.at[1]).wait()


def per_device(levels, members, state, noise, cot, shift, visc, ns, w_in, b_in, w_mid, b_mid, w_out):
    shape = state.shape
    lat_count, lon_count = shape[3:]
    fields = shape[0] * shape[1] * shape[2]
    hidden = w_in.shape[1]
    blocks = lat_count // 32
    waves = 2 * WAVES
    flat = (fields, lat_count, lon_count)
    own = hidden // levels // members
    smem = pl.BlockSpec(memory_space=pltpu.SMEM)
    hbm = pl.BlockSpec(memory_space=pl.ANY)
    vmem = pl.BlockSpec(memory_space=pltpu.VMEM)
    dma = pltpu.SemaphoreType.DMA
    out = pl.pallas_call(
        functools.partial(kernel, levels, members, lat_count, lon_count, hidden),
        name="ensemble_step",
        out_shape=(
            jax.ShapeDtypeStruct(flat, F32),
            jax.ShapeDtypeStruct(flat, F32),
            jax.ShapeDtypeStruct((w_in.shape[0], own), F32),
            jax.ShapeDtypeStruct((hidden, own), F32),
            jax.ShapeDtypeStruct((w_out.shape[1], own), F32),
            jax.ShapeDtypeStruct((2, own), F32),
        ),
        in_specs=[smem] * 3 + [hbm] * 3 + [vmem] * 13,
        out_specs=(hbm, hbm, vmem, vmem, vmem, vmem),
        scratch_shapes=[
            pltpu.VMEM(flat, F32),
            pltpu.VMEM(flat, BF16),
            pltpu.VMEM(flat, BF16),
            pltpu.VMEM((blocks, levels, 16, lon_count), BF16),
            pltpu.VMEM((blocks, levels, 16, lon_count), BF16),
            pltpu.VMEM((blocks, levels, 16, waves), BF16),
            pltpu.VMEM((blocks, levels, 16, waves), BF16),
            pltpu.VMEM((blocks, levels, 16, lon_count + waves), BF16),
            pltpu.VMEM((blocks, levels, 16, lon_count + waves), BF16),
            pltpu.VMEM(flat, F32),
            pltpu.VMEM((fields, lat_count, waves), F32),
            pltpu.VMEM((waves // 128, lat_count * fields, 128), F32),
            pltpu.VMEM((lon_count // 128, 256, 128), F32),
            pltpu.VMEM(((lon_count + waves) // 128, 256, 128), F32),
            pltpu.VMEM((hidden, w_in.shape[0]), BF16),
            pltpu.VMEM((hidden, hidden), BF16),
            pltpu.VMEM((w_out.shape[1], hidden), BF16),
            pltpu.VMEM((hidden, 128), F32),
            pltpu.VMEM((hidden, 128), F32),
            pltpu.VMEM((fields, WAVES), F32),
            pltpu.VMEM((fields, WAVES), F32),
            pltpu.VMEM((hidden, 128), F32),
            pltpu.VMEM((hidden, hidden), F32),
            pltpu.VMEM((hidden, 128), F32),
            pltpu.VMEM((hidden, 128), F32),
            pltpu.VMEM((hidden, 128), F32),
            pltpu.VMEM((levels, 16, 1024), BF16),
            pltpu.VMEM((levels, 16, 1024), BF16),
            pltpu.VMEM((16, 1024), BF16),
            pltpu.VMEM((members, 16, 1024), BF16),
            dma((3,)),
            dma((2,)),
            dma(()),
            dma(()),
            dma(()),
            dma(()),
            dma(()),
            dma((blocks,)),
            dma(()),
            dma(()),
            dma(()),
            dma(()),
        ],
        compiler_params=pltpu.CompilerParams(
            collective_id=0, has_side_effects=True, vmem_limit_bytes=60 << 20
        ),
    )(
        shift, visc, ns, state.reshape(flat), noise.reshape(flat), cot.reshape(flat),
        w_in, b_in.reshape(1, -1), w_mid, b_mid.reshape(1, -1), w_out,
        *[jnp.asarray(t) for t in tables(lat_count, lon_count)],
    )
    return (out[0].reshape(shape), out[1].reshape(shape), *out[2:])


def solution(mesh):
    grid = P("member", "level", None, None, None)
    return jax.shard_map(
        functools.partial(per_device, mesh.shape["level"], mesh.shape["member"]),
        mesh=mesh,
        in_specs=(grid, grid, grid, P("level", None), P("level", None), P("level", None))
        + (P(),) * 5,
        out_specs=(grid, grid) + (P(None, ("level", "member")),) * 4,
        check_vma=False,
    )
```

```python
import functools
import math

import jax
import jax.numpy as jnp
import ml_dtypes
import numpy as np
from jax import lax
from jax.experimental import pallas as pl
from jax.experimental.pallas import tpu as pltpu
from jax.sharding import PartitionSpec as P

WAVES = 128
MODES = 128
F32 = jnp.float32
BF16 = jnp.bfloat16
MESH = pl.DeviceIdType.MESH
EARLY = 3
VMEM_LIMIT = 46 << 20


def halves_np(table):
    high = table.astype(ml_dtypes.bfloat16)
    low = (table - high.astype(np.float64)).astype(ml_dtypes.bfloat16)
    return high, low


def tables(lat_count, lon_count):
    lon = np.arange(lon_count)[:, None] * np.arange(WAVES)[None, :] % lon_count
    phase = 2.0 * np.pi * lon / lon_count
    lon_fwd = np.concatenate([np.cos(phase), np.sin(phase)], axis=1)
    turn = (2 * np.arange(lat_count)[:, None] + 1) * np.arange(MODES)[None, :] % (4 * lat_count)
    lat_fwd = np.cos(np.pi * turn / (2 * lat_count))
    out = []
    for table in (lon_fwd, lon_fwd.T, lat_fwd, lat_fwd.T):
        out.extend(halves_np(np.ascontiguousarray(table)))
    return out


def unit_order(hidden, levels, members):
    columns = members // 2
    units = np.arange(hidden).reshape(levels, 2, columns, -1)
    order = units.transpose(2, 0, 1, 3).reshape(-1)
    return (order[:, None] == np.arange(hidden)[None, :]).astype(ml_dtypes.bfloat16)


def halves(x):
    high = x.astype(BF16)
    return high, (x - high.astype(F32)).astype(BF16)


def dot(a, b):
    return jnp.dot(a, b, preferred_element_type=F32)


def dot_nt(a, b):
    return lax.dot_general(a, b, (((1,), (1,)), ((), ())), preferred_element_type=F32)


def dot3(a, b):
    return dot(a[0], b[0]) + dot(a[0], b[1]) + dot(a[1], b[0])


def put_rows(ref, rows, x):
    for c in range(x.shape[1] // 128):
        ref[c, rows, :] = x[:, c * 128 : (c + 1) * 128]


def get_rows(ref, rows, first, count):
    return jnp.concatenate([ref[c, rows, :] for c in range(first, first + count)], axis=1)


def sigmoid(x):
    return 0.5 * jnp.tanh(0.5 * x) + 0.5


def kernel(
    levels, members, lat_count, lon_count, hidden,
    shift_ref, visc_ref, ns_ref, state_hbm, noise_hbm, cot_hbm,
    w_in_hbm, w_mid_hbm, w_out_hbm, lfh_hbm, lfl_hbm, lth_hbm, ltl_hbm, lah_hbm, lal_hbm, ath_hbm, atl_hbm,
    order_hbm, b_in_hbm, b_mid_hbm,
    next_v, grad_v, sums_ref,
    w_in_v, w_mid_v, w_out_v, lfh_ref, lfl_ref, lth_ref, ltl_ref, lah_ref, lal_ref, ath_ref, atl_ref,
    order_ref, b_in_ref, b_mid_ref,
    w_in_ref, w_mid_ref, w_out_ref,
    state_v, noise_v, cot_v, g16, rg, h16, rh, tb, tbr, bb, bbr, z_v, h32, st_v, t_v, b_v,
    win_t, wmid_t, wout_t, bb1, bb2, cs_v, sn_v, gi_a, gm_a, go_a, s1_a, s2_a,
    gs, gx, gl, gr, ms, mr,
    in_sem, state_sem, w_sem, g_send, g_recv, h_send, h_recv, t_send, t_recv, b_send, b_recv,
    x_send, x_recv, s_send, s_recv, m_send, m_recv,
):
    me = lax.axis_index("level")
    mem = lax.axis_index("member")
    blocks = lat_count // 32
    fields = 8
    waves = 2 * WAVES
    lon_tiles = lon_count // 128
    wave_tiles = waves // 128

    def load_block(a):
        rows = pl.ds(pl.multiple_of(a * 32, 32), 32)
        return (
            pltpu.make_async_copy(noise_hbm.at[:, rows], noise_v.at[:, rows], in_sem.at[0, a]),
            pltpu.make_async_copy(cot_hbm.at[:, rows], cot_v.at[:, rows], in_sem.at[1, a]),
        )

    for a in range(blocks):
        for copy in load_block(a):
            copy.start()
    load_state = pltpu.make_async_copy(state_hbm, state_v, state_sem)
    load_state.start()
    given = [
        pltpu.make_async_copy(src, dst, w_sem.at[i])
        for i, (src, dst) in enumerate(
            [
                (lfh_hbm, lfh_ref), (lfl_hbm, lfl_ref), (ath_hbm, ath_ref), (atl_hbm, atl_ref),
                (lah_hbm, lah_ref), (lal_hbm, lal_ref), (lth_hbm, lth_ref), (ltl_hbm, ltl_ref),
                (w_in_hbm, w_in_v), (w_mid_hbm, w_mid_v), (w_out_hbm, w_out_v), (order_hbm, order_ref),
                (b_in_hbm, b_in_ref), (b_mid_hbm, b_mid_ref),
            ]
        )
    ]
    for copy in given:
        copy.start()

    barrier = pltpu.get_barrier_semaphore()

    def greet_level(d, _):
        pl.semaphore_signal(
            barrier, inc=1, device_id={"level": lax.rem(me + d, levels)}, device_id_type=MESH
        )
        return 0

    columns_x = members // 2
    my_y, my_x = mem // columns_x, lax.rem(mem, columns_x)
    beside = [my_y * columns_x + lax.rem(my_x + d, columns_x) for d in range(1, columns_x)]
    across = (1 - my_y) * columns_x + my_x

    lax.fori_loop(1, levels, greet_level, 0)
    for to in (*beside, across):
        pl.semaphore_signal(barrier, inc=1, device_id={"member": to}, device_id_type=MESH)
    pl.semaphore_wait(barrier, levels - 1 + columns_x)

    def send_level(src, dst, send, recv):
        def one(d, _):
            to = lax.rem(me + d, levels)
            pltpu.make_async_remote_copy(
                src(to), dst, send, recv, device_id={"level": to}, device_id_type=MESH
            ).start()
            return 0

        lax.fori_loop(1, levels, one, 0)

    mine = pl.ds(me, 1)

    def noise_scale(f):
        return ns_ref[f // 4, f % 4]

    def make_grad(a, _):
        for copy in load_block(a):
            copy.wait()
        rows = pl.ds(pl.multiple_of(a * 32, 32), 32)
        for f in range(fields):
            factor = 1.0 + noise_scale(f) * noise_v[f, rows, :].astype(F32)
            put_rows(st_v, pl.ds(f, 32, stride=fields), cot_v[f, rows, :].astype(F32) * factor)
        g16[a] = get_rows(st_v, slice(None), 0, lon_tiles).astype(BF16).reshape(levels, 16, lon_count)
        send_level(lambda to: g16.at[a, pl.ds(to, 1)], rg.at[a, mine], g_send, g_recv.at[a])
        rg[a, mine] = g16[a, mine]
        return 0

    lax.fori_loop(0, blocks, make_grad, 0)

    field_row = lax.broadcasted_iota(jnp.int32, (fields, WAVES), 0)
    wave = lax.broadcasted_iota(jnp.int32, (fields, WAVES), 1).astype(F32)
    shift = jnp.zeros((fields, WAVES), F32)
    for f in range(fields):
        shift = jnp.where(field_row == f, shift_ref[f // 4, f % 4], shift)
    cs_v[...] = jnp.cos(shift * wave)
    sn_v[...] = jnp.sin(shift * wave)
    p_index = lax.broadcasted_iota(jnp.int32, (MODES, WAVES), 0).astype(F32)
    k_index = lax.broadcasted_iota(jnp.int32, (MODES, WAVES), 1).astype(F32)
    radial = (k_index / WAVES) ** 2 + (p_index / MODES) ** 2
    weight = (
        jnp.where(p_index == 0, 1.0, 2.0) / lat_count * (jnp.where(k_index == 0, 1.0, 2.0) / lon_count)
    )

    def rotation(f):
        damping = jnp.exp(-visc_ref[f // 4, f % 4] * radial) * weight
        return cs_v[pl.ds(f, 1), :] * damping, sn_v[pl.ds(f, 1), :] * damping

    lf = (lfh_ref, lfl_ref)
    lt = (lth_ref, ltl_ref)
    la = (lah_ref, lal_ref)
    at = (ath_ref, atl_ref)

    def both(pair):
        return pair[0][...], pair[1][...]

    load_state.wait()
    for copy in given[:6]:
        copy.wait()

    def forward(f, _):
        partial = halves(dot3(halves(state_v[f]), both(lf)))
        spectrum = dot3(both(at), partial)
        cosine, sine = rotation(f)
        a, b = spectrum[:, :WAVES], spectrum[:, WAVES:]
        rotated = jnp.concatenate([a * cosine - b * sine, a * sine + b * cosine], axis=1)
        put_rows(h32, pl.ds(f, lat_count, stride=fields), dot3(both(la), halves(rotated)))
        return 0

    lax.fori_loop(0, fields, forward, 0)

    def pack_rows(b, _):
        for r in range(2):
            rows = pl.ds(pl.multiple_of(b * 512, 512) + 256 * r, 256)
            packed = get_rows(h32, rows, 0, wave_tiles).astype(BF16)
            h16[2 * b + r] = packed.reshape(levels, 16, waves)
        two = pl.ds(2 * b, 2)
        send_level(lambda to: h16.at[two, pl.ds(to, 1)], rh.at[two, mine], h_send, h_recv.at[b])
        rh[two, mine] = h16[two, mine]
        return 0

    lax.fori_loop(0, blocks // 2, pack_rows, 0)

    for copy in given[6:]:
        copy.wait()

    order = order_ref[...]

    def units_first(bias_ref):
        bias = jnp.broadcast_to(bias_ref[...].reshape(1, hidden), (128, hidden)).T
        high, rest = halves(bias)
        mid, low = halves(bias - high.astype(F32))
        return dot(order, high) + dot(order, mid) + dot(order, low)

    win_t[...] = dot_nt(order, w_in_v[...]).astype(BF16)
    w_in_ref[...] = dot_nt(w_in_v[...], order).astype(BF16)
    w_mid_ref[...] = dot_nt(dot(order, w_mid_v[...]).astype(BF16), order).astype(BF16)
    wmid_t[...] = dot_nt(dot_nt(order, w_mid_v[...]).astype(BF16), order).astype(BF16)
    w_out = dot(order, w_out_v[...])
    w_out_ref[...] = w_out.astype(BF16)
    wout_t[...] = w_out.T.astype(BF16)
    bb1[...] = units_first(b_in_ref)
    bb2[...] = units_first(b_mid_ref)
    gi_a[...] = jnp.zeros_like(gi_a)
    gm_a[...] = jnp.zeros_like(gm_a)
    go_a[...] = jnp.zeros_like(go_a)
    s1_a[...] = jnp.zeros_like(s1_a)
    s2_a[...] = jnp.zeros_like(s2_a)

    def local(f, _):
        rows = get_rows(h32, pl.ds(f, lat_count, stride=fields), 0, wave_tiles)
        next_v[f] = dot3(halves(rows), both(lt))
        cot = cot_v[f]
        z_v[f] = dot(cot, lfh_ref[...]) + dot(cot, lfl_ref[...])
        return 0

    lax.fori_loop(0, fields, local, 0)

    others = pl.ds(0, levels - 1)

    def wait_for(ref, sem):
        pltpu.make_async_copy(ref, ref, sem).wait()


    def lanes(x):
        x = x.reshape(levels, 2, 8, lon_count)
        return jnp.concatenate(
            [x[:, r].reshape(levels * 8, lon_count) for r in range(2)], axis=1
        ).astype(BF16)

    def rows_of(x0, x1, width):
        parts = [x.reshape(levels, 8, width) for x in (x0, x1)]
        return jnp.concatenate(parts, axis=1).astype(BF16)

    def lane_sum(x):
        out = x[:, :128]
        for c in range(1, x.shape[1] // 128):
            out = out + x[:, c * 128 : (c + 1) * 128]
        return out

    cols = 2 * lon_count

    def columns(a, _):
        wait_for(rg.at[a, others], g_recv.at[a])

        @pl.when(lax.rem(a, 2) == 0)
        def _():
            wait_for(rh.at[pl.ds(a, 2), others], h_recv.at[a // 2])

        spec = rh[a].reshape(levels * 16, waves)
        inp = lanes(dot(spec, lth_ref[...]) + dot(spec, ltl_ref[...]))
        gt = lanes(rg[a].reshape(levels * 16, lon_count).astype(F32))
        pre = dot(win_t[...], inp) + jnp.tile(bb1[...], (1, cols // 128))
        sg = sigmoid(pre)
        act = pre * sg
        slope1 = sg + act * (1.0 - sg)
        act1 = act.astype(BF16)
        pre = dot(wmid_t[...], act1) + jnp.tile(bb2[...], (1, cols // 128))
        sg = sigmoid(pre)
        act = pre * sg
        slope2 = sg + act * (1.0 - sg)
        act2 = act.astype(BF16)
        tend = dot(wout_t[...], act2)
        tb[a] = rows_of(tend[:, :lon_count], tend[:, lon_count:], lon_count)
        go_a[...] += dot_nt(act2, gt)
        slope = dot(w_out_ref[...], gt) * slope2
        s2_a[...] += lane_sum(slope)
        s2 = slope.astype(BF16)
        gm_a[...] += dot_nt(s2, act1)
        slope = dot(w_mid_ref[...], s2) * slope1
        s1_a[...] += lane_sum(slope)
        s1 = slope.astype(BF16)
        gi_a[...] += dot_nt(s1, inp)
        back = dot(w_in_ref[...], s1).astype(BF16)
        back = jnp.concatenate([back[:, :lon_count], back[:, lon_count:]], axis=0)
        back = dot(back, lfh_ref[...]) + dot(back, lfl_ref[...])
        half = levels * 8
        bb[a] = rows_of(back[:half], back[half:], waves)

        @pl.when(lax.rem(a, 2) == 1)
        def _():
            two = pl.ds(a - 1, 2)
            send_level(lambda to: bb.at[two, pl.ds(to, 1)], bbr.at[two, mine], b_send, b_recv)
            bbr[two, mine] = bb[two, mine]

        @pl.when(a < EARLY)
        def _():
            send_tend(a, 0)

        return 0

    def send_tend(a, _):
        send_level(lambda to: tb.at[a, pl.ds(to, 1)], tbr.at[a, mine], t_send, t_recv.at[a])
        tbr[a, mine] = tb[a, mine]
        return 0

    lax.fori_loop(0, blocks, columns, 0)

    lane = lax.broadcasted_iota(jnp.int32, (hidden, 128), 1)
    bias = jnp.where(lane == 0, jnp.sum(s1_a[...], axis=1, keepdims=True), 0.0)
    bias = jnp.where(lane == 1, jnp.sum(s2_a[...], axis=1, keepdims=True), bias)
    parts = [gi_a[...].astype(BF16), dot(gm_a[...].astype(BF16), order).astype(BF16)]
    parts += [go_a[...].astype(BF16), bias.astype(BF16)]
    gs[...] = jnp.concatenate(parts, axis=1).reshape(columns_x, hidden // columns_x, 768)
    for d, to in enumerate(beside):
        pltpu.make_async_remote_copy(
            gs.at[lax.rem(my_x + d + 1, columns_x)], gx.at[my_x], x_send, x_recv,
            device_id={"member": to}, device_id_type=MESH,
        ).start()
    gx[my_x] = gs[my_x]
    lax.fori_loop(EARLY, EARLY + 2, send_tend, 0)

    wait_for(bbr.at[:, others], b_recv)

    def gather(a, _):
        put_rows(b_v, slice(None), bbr[a].astype(F32).reshape(256, waves))
        rows = pl.ds(pl.multiple_of(a * 32, 32), 32)
        for f in range(fields):
            z_v[f, rows, :] += get_rows(b_v, pl.ds(f, 32, stride=fields), 0, wave_tiles)
        return 0

    lax.fori_loop(0, blocks, gather, 0)

    def backward(f, _):
        spectrum = dot3(both(at), halves(z_v[f]))
        cosine, sine = rotation(f)
        a, b = spectrum[:, :WAVES], spectrum[:, WAVES:]
        turned = jnp.concatenate([a * cosine + b * sine, b * cosine - a * sine], axis=1)
        rows = halves(dot3(both(la), halves(turned)))
        grad_v[f] = dot3(rows, both(lt))
        late = EARLY + 2 + f // 2

        @pl.when((lax.rem(f, 2) == 0) & (late < blocks))
        def _():
            send_tend(late, 0)

        return 0

    lax.fori_loop(0, fields, backward, 0)

    wait_for(gx.at[pl.ds(0, columns_x - 1)], x_recv)
    total = gx[0].astype(F32)
    for s in range(1, columns_x):
        total = total + gx[s].astype(F32)
    total = total.astype(BF16)
    share = hidden // columns_x // levels
    place = lax.broadcasted_iota(jnp.int32, (levels * 8, hidden // columns_x), 0)
    unit = lax.broadcasted_iota(jnp.int32, (levels * 8, hidden // columns_x), 1)
    within = place & 7
    spread = jnp.where((unit == (place >> 3) * share + within) & (within < share), 1.0, 0.0).astype(BF16)
    pair = [dot(spread, total[:, c : c + 384]).reshape(levels, 8, 384) for c in (0, 384)]
    gl[...] = jnp.concatenate(pair, axis=1).astype(BF16)
    send_level(lambda to: gl.at[pl.ds(to, 1)], gr.at[mine], s_send, s_recv)
    gr[mine] = gl[mine]

    def arrive(a, _):
        wait_for(tbr.at[a, others], t_recv.at[a])
        put_rows(t_v, slice(None), tbr[a].astype(F32).reshape(256, lon_count))
        rows = pl.ds(pl.multiple_of(a * 32, 32), 32)
        for f in range(fields):
            factor = 1.0 + noise_scale(f) * noise_v[f, rows, :].astype(F32)
            next_v[f, rows, :] += get_rows(t_v, pl.ds(f, 32, stride=fields), 0, lon_tiles) * factor
        return 0

    lax.fori_loop(0, blocks - 3, arrive, 0)

    wait_for(gr.at[others], s_recv)
    total = gr[0].astype(F32)
    for s in range(1, levels):
        total = total + gr[s].astype(F32)
    ms[...] = total.astype(BF16)
    swap = pltpu.make_async_remote_copy(
        ms, mr, m_send, m_recv, device_id={"member": across}, device_id_type=MESH
    )
    swap.start()

    lax.fori_loop(blocks - 3, blocks, arrive, 0)

    swap.wait()
    norm = 1.0 / math.sqrt(members * lat_count * lon_count)
    sums_ref[...] = (total + mr[...].astype(F32)) * norm

    wait_for(g16.at[:, others], g_send)
    wait_for(h16.at[:, others], h_send)
    wait_for(tb.at[:, others], t_send)
    wait_for(bb.at[:, others], b_send)
    wait_for(gs.at[pl.ds(0, columns_x - 1)], x_send)
    wait_for(gl.at[others], s_send)


def finish(
    hidden, levels, members, next_in, grad_in, sums_ref, next_out, grad_out, gin_ref, gmid_ref,
    gout_ref, gbias_ref, sem,
):
    stores = []
    for i, (src, dst) in enumerate(((next_in, next_out), (grad_in, grad_out))):
        for f in range(src.shape[0]):
            stores.append(pltpu.make_async_copy(src.at[f], dst.at[f], sem.at[i, f]))
    for store in stores:
        store.start()
    own = hidden // levels // members
    first = lax.axis_index("member") // (members // 2) * own
    slot = lax.broadcasted_iota(jnp.int32, (8, 8), 0)
    unit = lax.broadcasted_iota(jnp.int32, (8, 8), 1)
    choose = jnp.where((unit == first + slot) & (slot < own), 1.0, 0.0)

    def exact(a, b, dims):
        return lax.dot_general(
            a, b, (dims, ((), ())), precision=lax.Precision.HIGHEST, preferred_element_type=F32
        )

    top = exact(choose, sums_ref[:8, :], ((1,), (0,)))
    low = exact(choose, sums_ref[8:, :], ((1,), (0,)))
    gin_ref[...] = top[:own, :128]
    gmid_ref[...] = jnp.concatenate([top[:, 128:], low[:, :128]], axis=1)[:own]
    gout_ref[...] = low[:own, 128:256]
    lane = lax.broadcasted_iota(jnp.int32, (8, 128), 1)
    row = lax.broadcasted_iota(jnp.int32, (8, 128), 0)
    take = jnp.where((lane == row) & (row < 2), 1.0, 0.0)
    gbias_ref[...] = exact(take, low[:, 256:], ((1,), (1,)))[:2, :own]
    for store in stores:
        store.wait()


def per_device(levels, members, state, noise, cot, shift, visc, ns, w_in, b_in, w_mid, b_mid, w_out):
    shape = state.shape
    lat_count, lon_count = shape[3:]
    fields = shape[0] * shape[1] * shape[2]
    hidden = w_in.shape[1]
    blocks = lat_count // 32
    waves = 2 * WAVES
    flat = (fields, lat_count, lon_count)
    own = hidden // levels // members
    smem = pl.BlockSpec(memory_space=pltpu.SMEM)
    hbm = pl.BlockSpec(memory_space=pl.ANY)
    vmem = pl.BlockSpec(memory_space=pltpu.VMEM)
    dma = pltpu.SemaphoreType.DMA
    given = [w_in, w_mid, w_out, *[jnp.asarray(t) for t in tables(lat_count, lon_count)]]
    given += [jnp.asarray(unit_order(hidden, levels, members)), b_in, b_mid]
    grid_rows = pltpu.VMEM((blocks, levels, 16, lon_count), BF16)
    wave_rows = pltpu.VMEM((blocks, levels, 16, waves), BF16)
    per_unit = pltpu.VMEM((hidden, 128), F32)
    state_out, grad_out, sums = pl.pallas_call(
        functools.partial(kernel, levels, members, lat_count, lon_count, hidden),
        name="ensemble_step",
        out_shape=(
            pltpu.VMEM(flat, F32),
            pltpu.VMEM(flat, F32),
            pltpu.VMEM((16, 384), F32),
        ),
        in_specs=[smem] * 3 + [hbm] * (3 + len(given)),
        out_specs=(vmem, vmem, vmem),
        scratch_shapes=[pltpu.VMEM(x.shape, x.dtype) for x in given]
        + [pltpu.VMEM(x.shape, BF16) for x in given[:3]]
        + [
            pltpu.VMEM(flat, F32),
            pltpu.VMEM(flat, BF16),
            pltpu.VMEM(flat, BF16),
            grid_rows, grid_rows, wave_rows, wave_rows, grid_rows, grid_rows, wave_rows, wave_rows,
            pltpu.VMEM((fields, lat_count, waves), F32),
            pltpu.VMEM((waves // 128, lat_count * fields, 128), F32),
            pltpu.VMEM((lon_count // 128, 256, 128), F32),
            pltpu.VMEM((lon_count // 128, 256, 128), F32),
            pltpu.VMEM((waves // 128, 256, 128), F32),
            pltpu.VMEM((hidden, w_in.shape[0]), BF16),
            pltpu.VMEM((hidden, hidden), BF16),
            pltpu.VMEM((w_out.shape[1], hidden), BF16),
            per_unit, per_unit,
            pltpu.VMEM((fields, WAVES), F32),
            pltpu.VMEM((fields, WAVES), F32),
            per_unit,
            pltpu.VMEM((hidden, hidden), F32),
            per_unit, per_unit, per_unit,
            pltpu.VMEM((members // 2, hidden // (members // 2), 768), BF16),
            pltpu.VMEM((members // 2, hidden // (members // 2), 768), BF16),
            pltpu.VMEM((levels, 16, 384), BF16),
            pltpu.VMEM((levels, 16, 384), BF16),
            pltpu.VMEM((16, 384), BF16),
            pltpu.VMEM((16, 384), BF16),
            dma((2, blocks)), dma(()), dma((len(given),)),
            dma(()), dma((blocks,)), dma(()), dma((blocks // 2,)), dma(()), dma((blocks,)),
            dma(()), dma(()), dma(()), dma(()), dma(()), dma(()), dma(()), dma(()),
        ],
        compiler_params=pltpu.CompilerParams(
            collective_id=0, has_side_effects=True, vmem_limit_bytes=VMEM_LIMIT
        ),
    )(
        shift, visc, ns,
        *[pltpu.with_memory_space_constraint(x, pltpu.HBM)
          for x in (state.reshape(flat), noise.reshape(flat), cot.reshape(flat), *given)],
    )
    out = pl.pallas_call(
        functools.partial(finish, hidden, levels, members),
        name="finish",
        out_shape=(
            jax.ShapeDtypeStruct(flat, F32),
            jax.ShapeDtypeStruct(flat, F32),
            jax.ShapeDtypeStruct((own, w_in.shape[0]), F32),
            jax.ShapeDtypeStruct((own, hidden), F32),
            jax.ShapeDtypeStruct((own, w_out.shape[1]), F32),
            jax.ShapeDtypeStruct((2, own), F32),
        ),
        in_specs=[vmem, vmem, vmem],
        out_specs=(hbm, hbm, vmem, vmem, vmem, vmem),
        scratch_shapes=[dma((2, fields))],
        compiler_params=pltpu.CompilerParams(vmem_limit_bytes=32 << 20),
    )(state_out, grad_out, sums)
    return (
        out[0].reshape(shape), out[1].reshape(shape), out[2].T, out[3].T, out[4].T, out[5],
    )


def solution(mesh):
    grid = P("member", "level", None, None, None)
    return jax.shard_map(
        functools.partial(per_device, mesh.shape["level"], mesh.shape["member"]),
        mesh=mesh,
        in_specs=(grid, grid, grid, P("level", None), P("level", None), P("level", None))
        + (P(),) * 5,
        out_specs=(grid, grid) + (P(None, ("level", "member")),) * 4,
        check_vma=False,
    )
```

```python
import functools
import math

import jax
import jax.numpy as jnp
import ml_dtypes
import numpy as np
from jax import lax
from jax.experimental import pallas as pl
from jax.experimental.pallas import tpu as pltpu
from jax.sharding import PartitionSpec as P

WAVES = 128
MODES = 128
F32 = jnp.float32
BF16 = jnp.bfloat16
MESH = pl.DeviceIdType.MESH
EARLY = 2
STRIDE = 7
VMEM_LIMIT = 46 << 20


def halves_np(table):
    high = table.astype(ml_dtypes.bfloat16)
    low = (table - high.astype(np.float64)).astype(ml_dtypes.bfloat16)
    return high, low


def tables(lat_count, lon_count):
    lon = np.arange(lon_count)[:, None] * np.arange(WAVES)[None, :] % lon_count
    phase = 2.0 * np.pi * lon / lon_count
    lon_fwd = np.concatenate([np.cos(phase), np.sin(phase)], axis=1)
    turn = (2 * np.arange(lat_count)[:, None] + 1) * np.arange(MODES)[None, :] % (4 * lat_count)
    lat_fwd = np.cos(np.pi * turn / (2 * lat_count))
    out = []
    for table in (lon_fwd, lon_fwd.T, lat_fwd, lat_fwd.T):
        out.extend(halves_np(np.ascontiguousarray(table)))
    return out


def unit_order(hidden, levels, members):
    columns = members // 2
    units = np.arange(hidden).reshape(levels, 2, columns, -1)
    order = units.transpose(2, 0, 1, 3).reshape(-1)
    return (order[:, None] == np.arange(hidden)[None, :]).astype(ml_dtypes.bfloat16)


def halves(x):
    high = x.astype(BF16)
    return high, (x - high.astype(F32)).astype(BF16)


def dot(a, b):
    return jnp.dot(a, b, preferred_element_type=F32)


def dot_nt(a, b):
    return lax.dot_general(a, b, (((1,), (1,)), ((), ())), preferred_element_type=F32)


def dot3(a, b):
    return dot(a[0], b[0]) + dot(a[0], b[1]) + dot(a[1], b[0])


def put_rows(ref, rows, x):
    for c in range(x.shape[1] // 128):
        ref[c, rows, :] = x[:, c * 128 : (c + 1) * 128]


def get_rows(ref, rows, first, count):
    return jnp.concatenate([ref[c, rows, :] for c in range(first, first + count)], axis=1)


def sigmoid(x):
    return 0.5 * jnp.tanh(0.5 * x) + 0.5


def kernel(
    levels, members, lat_count, lon_count, hidden,
    shift_ref, visc_ref, ns_ref, state_hbm, noise_hbm, cot_hbm,
    w_in_hbm, w_mid_hbm, w_out_hbm, lfh_hbm, lfl_hbm, lth_hbm, ltl_hbm, lah_hbm, lal_hbm, ath_hbm, atl_hbm,
    order_hbm, b_in_hbm, b_mid_hbm,
    next_v, grad_v, sums_ref,
    w_in_v, w_mid_v, w_out_v, lfh_ref, lfl_ref, lth_ref, ltl_ref, lah_ref, lal_ref, ath_ref, atl_ref,
    order_ref, b_in_ref, b_mid_ref,
    w_in_ref, w_mid_ref, w_out_ref,
    state_v, noise_v, cot_v, g16, rg, h16, rh, tb, tbr, bb, bbr, z_v, h32, st_v, t_v, b_v,
    win_t, wmid_t, wout_t, bb1, bb2, cs_v, sn_v, gi_a, gm_a, go_a, s1_a, s2_a,
    gs, gx, gl, gr, ms, mr,
    in_sem, state_sem, w_sem, g_send, g_recv, h_send, h_recv, t_send, t_recv, b_send, b_recv,
    x_send, x_recv, s_send, s_recv, m_send, m_recv,
):
    me = lax.axis_index("level")
    mem = lax.axis_index("member")
    blocks = lat_count // 32
    fields = 8
    waves = 2 * WAVES
    lon_tiles = lon_count // 128
    wave_tiles = waves // 128

    def load_block(a):
        rows = pl.ds(pl.multiple_of(a * 32, 32), 32)
        return (
            pltpu.make_async_copy(noise_hbm.at[:, rows], noise_v.at[:, rows], in_sem.at[0, a]),
            pltpu.make_async_copy(cot_hbm.at[:, rows], cot_v.at[:, rows], in_sem.at[1, a]),
        )

    for copy in load_block(0):
        copy.start()

    barrier = pltpu.get_barrier_semaphore()

    def greet_level(d, _):
        pl.semaphore_signal(
            barrier, inc=1, device_id={"level": lax.rem(me + d, levels)}, device_id_type=MESH
        )
        return 0

    columns_x = members // 2
    my_y, my_x = mem // columns_x, lax.rem(mem, columns_x)
    beside = [my_y * columns_x + lax.rem(my_x + d, columns_x) for d in range(1, columns_x)]
    across = (1 - my_y) * columns_x + my_x

    lax.fori_loop(1, levels, greet_level, 0)
    for to in (*beside, across):
        pl.semaphore_signal(barrier, inc=1, device_id={"member": to}, device_id_type=MESH)

    for a in range(1, blocks):
        for copy in load_block(a):
            copy.start()
    load_state = pltpu.make_async_copy(state_hbm, state_v, state_sem)
    load_state.start()
    given = [
        pltpu.make_async_copy(src, dst, w_sem.at[i])
        for i, (src, dst) in enumerate(
            [
                (lfh_hbm, lfh_ref), (lfl_hbm, lfl_ref), (ath_hbm, ath_ref), (atl_hbm, atl_ref),
                (lah_hbm, lah_ref), (lal_hbm, lal_ref), (lth_hbm, lth_ref), (ltl_hbm, ltl_ref),
                (w_in_hbm, w_in_v), (w_mid_hbm, w_mid_v), (w_out_hbm, w_out_v), (order_hbm, order_ref),
                (b_in_hbm, b_in_ref), (b_mid_hbm, b_mid_ref),
            ]
        )
    ]
    for copy in given:
        copy.start()

    def send_level(src, dst, send, recv):
        def one(d, _):
            to = lax.rem(me + STRIDE * d, levels)
            pltpu.make_async_remote_copy(
                src(to), dst, send, recv, device_id={"level": to}, device_id_type=MESH
            ).start()
            return 0

        lax.fori_loop(1, levels, one, 0)

    mine = pl.ds(me, 1)

    def noise_scale(f):
        return ns_ref[f // 4, f % 4]

    def make_grad(a, _):
        for copy in load_block(a):
            copy.wait()
        rows = pl.ds(pl.multiple_of(a * 32, 32), 32)
        for f in range(fields):
            factor = 1.0 + noise_scale(f) * noise_v[f, rows, :].astype(F32)
            put_rows(st_v, pl.ds(f, 32, stride=fields), cot_v[f, rows, :].astype(F32) * factor)
        g16[a] = get_rows(st_v, slice(None), 0, lon_tiles).astype(BF16).reshape(levels, 16, lon_count)
        return 0

    def send_grad(a, _):
        send_level(lambda to: g16.at[a, pl.ds(to, 1)], rg.at[a, mine], g_send, g_recv.at[a])
        rg[a, mine] = g16[a, mine]
        return 0

    def deal_grad(a, _):
        make_grad(a, 0)
        return send_grad(a, 0)

    half = blocks // 2
    make_grad(0, 0)
    pl.semaphore_wait(barrier, levels - 1 + columns_x)
    send_grad(0, 0)
    lax.fori_loop(1, half, deal_grad, 0)

    field_row = lax.broadcasted_iota(jnp.int32, (fields, WAVES), 0)
    wave = lax.broadcasted_iota(jnp.int32, (fields, WAVES), 1).astype(F32)
    shift = jnp.zeros((fields, WAVES), F32)
    for f in range(fields):
        shift = jnp.where(field_row == f, shift_ref[f // 4, f % 4], shift)
    cs_v[...] = jnp.cos(shift * wave)
    sn_v[...] = jnp.sin(shift * wave)
    p_index = lax.broadcasted_iota(jnp.int32, (MODES, WAVES), 0).astype(F32)
    k_index = lax.broadcasted_iota(jnp.int32, (MODES, WAVES), 1).astype(F32)
    radial = (k_index / WAVES) ** 2 + (p_index / MODES) ** 2
    weight = (
        jnp.where(p_index == 0, 1.0, 2.0) / lat_count * (jnp.where(k_index == 0, 1.0, 2.0) / lon_count)
    )

    def rotation(f):
        damping = jnp.exp(-visc_ref[f // 4, f % 4] * radial) * weight
        return cs_v[pl.ds(f, 1), :] * damping, sn_v[pl.ds(f, 1), :] * damping

    lf = (lfh_ref, lfl_ref)
    lt = (lth_ref, ltl_ref)
    la = (lah_ref, lal_ref)
    at = (ath_ref, atl_ref)

    def both(pair):
        return pair[0][...], pair[1][...]

    load_state.wait()
    for copy in given[:6]:
        copy.wait()

    def forward(f, _):
        partial = halves(dot3(halves(state_v[f]), both(lf)))
        spectrum = dot3(both(at), partial)
        cosine, sine = rotation(f)
        a, b = spectrum[:, :WAVES], spectrum[:, WAVES:]
        rotated = jnp.concatenate([a * cosine - b * sine, a * sine + b * cosine], axis=1)
        put_rows(h32, pl.ds(f, lat_count, stride=fields), dot3(both(la), halves(rotated)))
        return 0

    lax.fori_loop(0, fields, forward, 0)

    def pack_rows(b, _):
        for r in range(2):
            rows = pl.ds(pl.multiple_of(b * 512, 512) + 256 * r, 256)
            packed = get_rows(h32, rows, 0, wave_tiles).astype(BF16)
            h16[2 * b + r] = packed.reshape(levels, 16, waves)
        two = pl.ds(2 * b, 2)
        send_level(lambda to: h16.at[two, pl.ds(to, 1)], rh.at[two, mine], h_send, h_recv.at[b])
        rh[two, mine] = h16[two, mine]
        return 0

    lax.fori_loop(0, half // 2, pack_rows, 0)

    def later(b, _):
        deal_grad(2 * b, 0)
        deal_grad(2 * b + 1, 0)
        return pack_rows(b, 0)

    lax.fori_loop(half // 2, half, later, 0)

    for copy in given[6:]:
        copy.wait()

    order = order_ref[...]

    def units_first(bias_ref):
        bias = jnp.broadcast_to(bias_ref[...].reshape(1, hidden), (128, hidden)).T
        high, rest = halves(bias)
        mid, low = halves(bias - high.astype(F32))
        return dot(order, high) + dot(order, mid) + dot(order, low)

    win_t[...] = dot_nt(order, w_in_v[...]).astype(BF16)
    w_in_ref[...] = dot_nt(w_in_v[...], order).astype(BF16)
    w_mid_ref[...] = dot_nt(dot(order, w_mid_v[...]).astype(BF16), order).astype(BF16)
    wmid_t[...] = dot_nt(dot_nt(order, w_mid_v[...]).astype(BF16), order).astype(BF16)
    w_out = dot(order, w_out_v[...])
    w_out_ref[...] = w_out.astype(BF16)
    wout_t[...] = w_out.T.astype(BF16)
    bb1[...] = units_first(b_in_ref)
    bb2[...] = units_first(b_mid_ref)
    gi_a[...] = jnp.zeros_like(gi_a)
    gm_a[...] = jnp.zeros_like(gm_a)
    go_a[...] = jnp.zeros_like(go_a)
    s1_a[...] = jnp.zeros_like(s1_a)
    s2_a[...] = jnp.zeros_like(s2_a)

    def local(f, _):
        rows = get_rows(h32, pl.ds(f, lat_count, stride=fields), 0, wave_tiles)
        next_v[f] = dot3(halves(rows), both(lt))
        cot = cot_v[f]
        z_v[f] = dot(cot, lfh_ref[...]) + dot(cot, lfl_ref[...])
        return 0

    others = pl.ds(0, levels - 1)

    def wait_for(ref, sem):
        pltpu.make_async_copy(ref, ref, sem).wait()


    def lanes(x):
        x = x.reshape(levels, 2, 8, lon_count)
        return jnp.concatenate(
            [x[:, r].reshape(levels * 8, lon_count) for r in range(2)], axis=1
        ).astype(BF16)

    def rows_of(x0, x1, width):
        parts = [x.reshape(levels, 8, width) for x in (x0, x1)]
        return jnp.concatenate(parts, axis=1).astype(BF16)

    def lane_sum(x):
        out = x[:, :128]
        for c in range(1, x.shape[1] // 128):
            out = out + x[:, c * 128 : (c + 1) * 128]
        return out

    cols = 2 * lon_count

    def columns(a, _):
        wait_for(rg.at[a, others], g_recv.at[a])

        @pl.when(lax.rem(a, 2) == 0)
        def _():
            wait_for(rh.at[pl.ds(a, 2), others], h_recv.at[a // 2])

        spec = rh[a].reshape(levels * 16, waves)
        inp = lanes(dot(spec, lth_ref[...]) + dot(spec, ltl_ref[...]))
        gt = lanes(rg[a].reshape(levels * 16, lon_count).astype(F32))
        pre = dot(win_t[...], inp) + jnp.tile(bb1[...], (1, cols // 128))
        sg = sigmoid(pre)
        act = pre * sg
        slope1 = sg + act * (1.0 - sg)
        act1 = act.astype(BF16)
        pre = dot(wmid_t[...], act1) + jnp.tile(bb2[...], (1, cols // 128))
        sg = sigmoid(pre)
        act = pre * sg
        slope2 = sg + act * (1.0 - sg)
        act2 = act.astype(BF16)
        tend = dot(wout_t[...], act2)
        tb[a] = rows_of(tend[:, :lon_count], tend[:, lon_count:], lon_count)
        go_a[...] += dot_nt(act2, gt)
        slope = dot(w_out_ref[...], gt) * slope2
        s2_a[...] += lane_sum(slope)
        s2 = slope.astype(BF16)
        gm_a[...] += dot_nt(s2, act1)
        slope = dot(w_mid_ref[...], s2) * slope1
        s1_a[...] += lane_sum(slope)
        s1 = slope.astype(BF16)
        gi_a[...] += dot_nt(s1, inp)
        back = dot(w_in_ref[...], s1).astype(BF16)
        back = jnp.concatenate([back[:, :lon_count], back[:, lon_count:]], axis=0)
        back = dot(back, lfh_ref[...]) + dot(back, lfl_ref[...])
        half = levels * 8
        bb[a] = rows_of(back[:half], back[half:], waves)

        @pl.when(lax.rem(a, 2) == 1)
        def _():
            two = pl.ds(a - 1, 2)
            send_level(lambda to: bb.at[two, pl.ds(to, 1)], bbr.at[two, mine], b_send, b_recv)
            bbr[two, mine] = bb[two, mine]

        @pl.when(a < EARLY)
        def _():
            send_tend(a, 0)

        return 0

    def send_tend(a, _):
        send_level(lambda to: tb.at[a, pl.ds(to, 1)], tbr.at[a, mine], t_send, t_recv.at[a])
        tbr[a, mine] = tb[a, mine]
        return 0

    lax.fori_loop(0, blocks, columns, 0)
    lax.fori_loop(EARLY, EARLY + 2, send_tend, 0)

    lane = lax.broadcasted_iota(jnp.int32, (hidden, 128), 1)
    bias = jnp.where(lane == 0, jnp.sum(s1_a[...], axis=1, keepdims=True), 0.0)
    bias = jnp.where(lane == 1, jnp.sum(s2_a[...], axis=1, keepdims=True), bias)
    parts = [gi_a[...].astype(BF16), dot(gm_a[...].astype(BF16), order).astype(BF16)]
    parts += [go_a[...].astype(BF16), bias.astype(BF16)]
    gs[...] = jnp.concatenate(parts, axis=1).reshape(columns_x, hidden // columns_x, 768)
    for d, to in enumerate(beside):
        pltpu.make_async_remote_copy(
            gs.at[lax.rem(my_x + d + 1, columns_x)], gx.at[my_x], x_send, x_recv,
            device_id={"member": to}, device_id_type=MESH,
        ).start()
    gx[my_x] = gs[my_x]
    lax.fori_loop(EARLY + 2, EARLY + 4, send_tend, 0)
    lax.fori_loop(0, fields, local, 0)

    wait_for(gx.at[pl.ds(0, columns_x - 1)], x_recv)
    total = gx[0].astype(F32)
    for s in range(1, columns_x):
        total = total + gx[s].astype(F32)
    total = total.astype(BF16)
    share = hidden // columns_x // levels
    place = lax.broadcasted_iota(jnp.int32, (levels * 8, hidden // columns_x), 0)
    unit = lax.broadcasted_iota(jnp.int32, (levels * 8, hidden // columns_x), 1)
    within = place & 7
    spread = jnp.where((unit == (place >> 3) * share + within) & (within < share), 1.0, 0.0).astype(BF16)
    pair = [dot(spread, total[:, c : c + 384]).reshape(levels, 8, 384) for c in (0, 384)]
    gl[...] = jnp.concatenate(pair, axis=1).astype(BF16)
    send_level(lambda to: gl.at[pl.ds(to, 1)], gr.at[mine], s_send, s_recv)
    gr[mine] = gl[mine]

    lax.fori_loop(EARLY + 4, EARLY + 5, send_tend, 0)

    wait_for(bbr.at[:, others], b_recv)

    def gather(a, _):
        put_rows(b_v, slice(None), bbr[a].astype(F32).reshape(256, waves))
        rows = pl.ds(pl.multiple_of(a * 32, 32), 32)
        for f in range(fields):
            z_v[f, rows, :] += get_rows(b_v, pl.ds(f, 32, stride=fields), 0, wave_tiles)
        return 0

    lax.fori_loop(0, blocks, gather, 0)

    def backward(f, _):
        spectrum = dot3(both(at), halves(z_v[f]))
        cosine, sine = rotation(f)
        a, b = spectrum[:, :WAVES], spectrum[:, WAVES:]
        turned = jnp.concatenate([a * cosine + b * sine, b * cosine - a * sine], axis=1)
        rows = halves(dot3(both(la), halves(turned)))
        grad_v[f] = dot3(rows, both(lt))
        late = EARLY + 5 + f // 2

        @pl.when((lax.rem(f, 2) == 0) & (late < blocks))
        def _():
            send_tend(late, 0)

        return 0

    lax.fori_loop(0, fields, backward, 0)

    def arrive(a, _):
        wait_for(tbr.at[a, others], t_recv.at[a])
        put_rows(t_v, slice(None), tbr[a].astype(F32).reshape(256, lon_count))
        rows = pl.ds(pl.multiple_of(a * 32, 32), 32)
        for f in range(fields):
            factor = 1.0 + noise_scale(f) * noise_v[f, rows, :].astype(F32)
            next_v[f, rows, :] += get_rows(t_v, pl.ds(f, 32, stride=fields), 0, lon_tiles) * factor
        return 0

    lax.fori_loop(0, blocks - 3, arrive, 0)

    wait_for(gr.at[others], s_recv)
    total = gr[0].astype(F32)
    for s in range(1, levels):
        total = total + gr[s].astype(F32)
    ms[...] = total.astype(BF16)
    swap = pltpu.make_async_remote_copy(
        ms, mr, m_send, m_recv, device_id={"member": across}, device_id_type=MESH
    )
    swap.start()

    lax.fori_loop(blocks - 3, blocks, arrive, 0)

    swap.wait()
    norm = 1.0 / math.sqrt(members * lat_count * lon_count)
    sums_ref[...] = (total + mr[...].astype(F32)) * norm

    wait_for(g16.at[:, others], g_send)
    wait_for(h16.at[:, others], h_send)
    wait_for(tb.at[:, others], t_send)
    wait_for(bb.at[:, others], b_send)
    wait_for(gs.at[pl.ds(0, columns_x - 1)], x_send)
    wait_for(gl.at[others], s_send)


def finish(
    hidden, levels, members, next_in, grad_in, sums_ref, next_out, grad_out, gin_ref, gmid_ref,
    gout_ref, gbias_ref, sem,
):
    stores = []
    for i, (src, dst) in enumerate(((next_in, next_out), (grad_in, grad_out))):
        for f in range(src.shape[0]):
            stores.append(pltpu.make_async_copy(src.at[f], dst.at[f], sem.at[i, f]))
    for store in stores:
        store.start()
    own = hidden // levels // members
    first = lax.axis_index("member") // (members // 2) * own
    slot = lax.broadcasted_iota(jnp.int32, (8, 8), 0)
    unit = lax.broadcasted_iota(jnp.int32, (8, 8), 1)
    choose = jnp.where((unit == first + slot) & (slot < own), 1.0, 0.0)

    def exact(a, b, dims):
        return lax.dot_general(
            a, b, (dims, ((), ())), precision=lax.Precision.HIGHEST, preferred_element_type=F32
        )

    top = exact(choose, sums_ref[:8, :], ((1,), (0,)))
    low = exact(choose, sums_ref[8:, :], ((1,), (0,)))
    gin_ref[...] = top[:own, :128]
    gmid_ref[...] = jnp.concatenate([top[:, 128:], low[:, :128]], axis=1)[:own]
    gout_ref[...] = low[:own, 128:256]
    lane = lax.broadcasted_iota(jnp.int32, (8, 128), 1)
    row = lax.broadcasted_iota(jnp.int32, (8, 128), 0)
    take = jnp.where((lane == row) & (row < 2), 1.0, 0.0)
    gbias_ref[...] = exact(take, low[:, 256:], ((1,), (1,)))[:2, :own]
    for store in stores:
        store.wait()


def per_device(levels, members, state, noise, cot, shift, visc, ns, w_in, b_in, w_mid, b_mid, w_out):
    shape = state.shape
    lat_count, lon_count = shape[3:]
    fields = shape[0] * shape[1] * shape[2]
    hidden = w_in.shape[1]
    blocks = lat_count // 32
    waves = 2 * WAVES
    flat = (fields, lat_count, lon_count)
    own = hidden // levels // members
    smem = pl.BlockSpec(memory_space=pltpu.SMEM)
    hbm = pl.BlockSpec(memory_space=pl.ANY)
    vmem = pl.BlockSpec(memory_space=pltpu.VMEM)
    dma = pltpu.SemaphoreType.DMA
    given = [w_in, w_mid, w_out, *[jnp.asarray(t) for t in tables(lat_count, lon_count)]]
    given += [jnp.asarray(unit_order(hidden, levels, members)), b_in, b_mid]
    grid_rows = pltpu.VMEM((blocks, levels, 16, lon_count), BF16)
    wave_rows = pltpu.VMEM((blocks, levels, 16, waves), BF16)
    per_unit = pltpu.VMEM((hidden, 128), F32)
    state_out, grad_out, sums = pl.pallas_call(
        functools.partial(kernel, levels, members, lat_count, lon_count, hidden),
        name="ensemble_step",
        out_shape=(
            pltpu.VMEM(flat, F32),
            pltpu.VMEM(flat, F32),
            pltpu.VMEM((16, 384), F32),
        ),
        in_specs=[smem] * 3 + [hbm] * (3 + len(given)),
        out_specs=(vmem, vmem, vmem),
        scratch_shapes=[pltpu.VMEM(x.shape, x.dtype) for x in given]
        + [pltpu.VMEM(x.shape, BF16) for x in given[:3]]
        + [
            pltpu.VMEM(flat, F32),
            pltpu.VMEM(flat, BF16),
            pltpu.VMEM(flat, BF16),
            grid_rows, grid_rows, wave_rows, wave_rows, grid_rows, grid_rows, wave_rows, wave_rows,
            pltpu.VMEM((fields, lat_count, waves), F32),
            pltpu.VMEM((waves // 128, lat_count * fields, 128), F32),
            pltpu.VMEM((lon_count // 128, 256, 128), F32),
            pltpu.VMEM((lon_count // 128, 256, 128), F32),
            pltpu.VMEM((waves // 128, 256, 128), F32),
            pltpu.VMEM((hidden, w_in.shape[0]), BF16),
            pltpu.VMEM((hidden, hidden), BF16),
            pltpu.VMEM((w_out.shape[1], hidden), BF16),
            per_unit, per_unit,
            pltpu.VMEM((fields, WAVES), F32),
            pltpu.VMEM((fields, WAVES), F32),
            per_unit,
            pltpu.VMEM((hidden, hidden), F32),
            per_unit, per_unit, per_unit,
            pltpu.VMEM((members // 2, hidden // (members // 2), 768), BF16),
            pltpu.VMEM((members // 2, hidden // (members // 2), 768), BF16),
            pltpu.VMEM((levels, 16, 384), BF16),
            pltpu.VMEM((levels, 16, 384), BF16),
            pltpu.VMEM((16, 384), BF16),
            pltpu.VMEM((16, 384), BF16),
            dma((2, blocks)), dma(()), dma((len(given),)),
            dma(()), dma((blocks,)), dma(()), dma((blocks // 2,)), dma(()), dma((blocks,)),
            dma(()), dma(()), dma(()), dma(()), dma(()), dma(()), dma(()), dma(()),
        ],
        compiler_params=pltpu.CompilerParams(
            collective_id=0, has_side_effects=True, vmem_limit_bytes=VMEM_LIMIT
        ),
    )(
        shift, visc, ns,
        *[pltpu.with_memory_space_constraint(x, pltpu.HBM)
          for x in (state.reshape(flat), noise.reshape(flat), cot.reshape(flat), *given)],
    )
    out = pl.pallas_call(
        functools.partial(finish, hidden, levels, members),
        name="finish",
        out_shape=(
            jax.ShapeDtypeStruct(flat, F32),
            jax.ShapeDtypeStruct(flat, F32),
            jax.ShapeDtypeStruct((own, w_in.shape[0]), F32),
            jax.ShapeDtypeStruct((own, hidden), F32),
            jax.ShapeDtypeStruct((own, w_out.shape[1]), F32),
            jax.ShapeDtypeStruct((2, own), F32),
        ),
        in_specs=[vmem, vmem, vmem],
        out_specs=(hbm, hbm, vmem, vmem, vmem, vmem),
        scratch_shapes=[dma((2, fields))],
        compiler_params=pltpu.CompilerParams(vmem_limit_bytes=32 << 20),
    )(state_out, grad_out, sums)
    return (
        out[0].reshape(shape), out[1].reshape(shape), out[2].T, out[3].T, out[4].T, out[5],
    )


def solution(mesh):
    grid = P("member", "level", None, None, None)
    return jax.shard_map(
        functools.partial(per_device, mesh.shape["level"], mesh.shape["member"]),
        mesh=mesh,
        in_specs=(grid, grid, grid, P("level", None), P("level", None), P("level", None))
        + (P(),) * 5,
        out_specs=(grid, grid) + (P(None, ("level", "member")),) * 4,
        check_vma=False,
    )
```

```python
import functools
import math

import jax
import jax.numpy as jnp
import ml_dtypes
import numpy as np
from jax import lax
from jax.experimental import pallas as pl
from jax.experimental.pallas import tpu as pltpu
from jax.sharding import PartitionSpec as P

WAVES = 128
MODES = 128
F32 = jnp.float32
BF16 = jnp.bfloat16
MESH = pl.DeviceIdType.MESH
EARLY = 2
STRIDE = 7
VMEM_LIMIT = 46 << 20


def halves_np(table):
    high = table.astype(ml_dtypes.bfloat16)
    low = (table - high.astype(np.float64)).astype(ml_dtypes.bfloat16)
    return high, low


def tables(lat_count, lon_count):
    lon = np.arange(lon_count)[:, None] * np.arange(WAVES)[None, :] % lon_count
    phase = 2.0 * np.pi * lon / lon_count
    lon_fwd = np.concatenate([np.cos(phase), np.sin(phase)], axis=1)
    turn = (2 * np.arange(lat_count)[:, None] + 1) * np.arange(MODES)[None, :] % (4 * lat_count)
    lat_fwd = np.cos(np.pi * turn / (2 * lat_count))
    out = []
    for table in (lon_fwd, lon_fwd.T, lat_fwd, lat_fwd.T):
        out.extend(halves_np(np.ascontiguousarray(table)))
    return out


def unit_order(hidden, levels, members):
    columns = members // 2
    units = np.arange(hidden).reshape(levels, 2, columns, -1)
    order = units.transpose(2, 0, 1, 3).reshape(-1)
    return (order[:, None] == np.arange(hidden)[None, :]).astype(ml_dtypes.bfloat16)


def halves(x):
    high = x.astype(BF16)
    return high, (x - high.astype(F32)).astype(BF16)


def dot(a, b):
    return jnp.dot(a, b, preferred_element_type=F32)


def dot_nt(a, b):
    return lax.dot_general(a, b, (((1,), (1,)), ((), ())), preferred_element_type=F32)


def dot3(a, b):
    return dot(a[0], b[0]) + dot(a[0], b[1]) + dot(a[1], b[0])


def put_rows(ref, rows, x):
    for c in range(x.shape[1] // 128):
        ref[c, rows, :] = x[:, c * 128 : (c + 1) * 128]


def get_rows(ref, rows, first, count):
    return jnp.concatenate([ref[c, rows, :] for c in range(first, first + count)], axis=1)


def sigmoid(x):
    return 0.5 * jnp.tanh(0.5 * x) + 0.5


def kernel(
    levels, members, lat_count, lon_count, hidden,
    shift_ref, visc_ref, ns_ref, state_hbm, noise_hbm, cot_hbm,
    w_in_hbm, w_mid_hbm, w_out_hbm, lfh_hbm, lfl_hbm, lth_hbm, ltl_hbm, lah_hbm, lal_hbm, ath_hbm, atl_hbm,
    order_hbm, b_in_hbm, b_mid_hbm,
    next_v, grad_v, sums_ref,
    w_in_v, w_mid_v, w_out_v, lfh_ref, lfl_ref, lth_ref, ltl_ref, lah_ref, lal_ref, ath_ref, atl_ref,
    order_ref, b_in_ref, b_mid_ref,
    w_in_ref, w_mid_ref, w_out_ref,
    state_v, noise_v, cot_v, g16, rg, h16, rh, tb, tbr, bb, bbr, z_v, h32, st_v, t_v, b_v,
    win_t, wmid_t, wout_t, bb1, bb2, cs_v, sn_v, gi_a, gm_a, go_a, s1_a, s2_a,
    gs, gx, gl, gr, ms, mr,
    in_sem, state_sem, w_sem, g_send, g_recv, h_send, h_recv, t_send, t_recv, b_send, b_recv,
    x_send, x_recv, s_send, s_recv, m_send, m_recv,
):
    me = lax.axis_index("level")
    mem = lax.axis_index("member")
    blocks = lat_count // 32
    fields = 8
    waves = 2 * WAVES
    lon_tiles = lon_count // 128
    wave_tiles = waves // 128

    def load_block(a):
        rows = pl.ds(pl.multiple_of(a * 32, 32), 32)
        return (
            pltpu.make_async_copy(noise_hbm.at[:, rows], noise_v.at[:, rows], in_sem.at[0, a]),
            pltpu.make_async_copy(cot_hbm.at[:, rows], cot_v.at[:, rows], in_sem.at[1, a]),
        )

    for copy in load_block(0):
        copy.start()

    barrier = pltpu.get_barrier_semaphore()

    def greet_level(d, _):
        pl.semaphore_signal(
            barrier, inc=1, device_id={"level": lax.rem(me + d, levels)}, device_id_type=MESH
        )
        return 0

    columns_x = members // 2
    my_y, my_x = mem // columns_x, lax.rem(mem, columns_x)
    beside = [my_y * columns_x + lax.rem(my_x + d, columns_x) for d in range(1, columns_x)]
    across = (1 - my_y) * columns_x + my_x

    for to in (*beside, across):
        pl.semaphore_signal(barrier, inc=1, device_id={"member": to}, device_id_type=MESH)
    lax.fori_loop(1, levels, greet_level, 0)

    for a in range(1, blocks):
        for copy in load_block(a):
            copy.start()
    load_state = pltpu.make_async_copy(state_hbm, state_v, state_sem)
    load_state.start()
    given = [
        pltpu.make_async_copy(src, dst, w_sem.at[i])
        for i, (src, dst) in enumerate(
            [
                (lfh_hbm, lfh_ref), (lfl_hbm, lfl_ref), (ath_hbm, ath_ref), (atl_hbm, atl_ref),
                (lah_hbm, lah_ref), (lal_hbm, lal_ref), (lth_hbm, lth_ref), (ltl_hbm, ltl_ref),
                (w_in_hbm, w_in_v), (w_mid_hbm, w_mid_v), (w_out_hbm, w_out_v), (order_hbm, order_ref),
                (b_in_hbm, b_in_ref), (b_mid_hbm, b_mid_ref),
            ]
        )
    ]
    for copy in given:
        copy.start()

    def send_level(src, dst, send, recv):
        def one(d, _):
            to = lax.rem(me + STRIDE * d, levels)
            pltpu.make_async_remote_copy(
                src(to), dst, send, recv, device_id={"level": to}, device_id_type=MESH
            ).start()
            return 0

        lax.fori_loop(1, levels, one, 0)

    mine = pl.ds(me, 1)

    def noise_scale(f):
        return ns_ref[f // 4, f % 4]

    def make_grad(a, _):
        for copy in load_block(a):
            copy.wait()
        rows = pl.ds(pl.multiple_of(a * 32, 32), 32)
        for f in range(fields):
            factor = 1.0 + noise_scale(f) * noise_v[f, rows, :].astype(F32)
            put_rows(st_v, pl.ds(f, 32, stride=fields), cot_v[f, rows, :].astype(F32) * factor)
        g16[a] = get_rows(st_v, slice(None), 0, lon_tiles).astype(BF16).reshape(levels, 16, lon_count)
        return 0

    def send_grad(a, _):
        send_level(lambda to: g16.at[a, pl.ds(to, 1)], rg.at[a, mine], g_send, g_recv.at[a])
        rg[a, mine] = g16[a, mine]
        return 0

    def deal_grad(a, _):
        make_grad(a, 0)
        return send_grad(a, 0)

    half = blocks // 2
    make_grad(0, 0)
    pl.semaphore_wait(barrier, levels - 1 + columns_x)
    send_grad(0, 0)
    lax.fori_loop(1, half, deal_grad, 0)

    field_row = lax.broadcasted_iota(jnp.int32, (fields, WAVES), 0)
    wave = lax.broadcasted_iota(jnp.int32, (fields, WAVES), 1).astype(F32)
    shift = jnp.zeros((fields, WAVES), F32)
    for f in range(fields):
        shift = jnp.where(field_row == f, shift_ref[f // 4, f % 4], shift)
    cs_v[...] = jnp.cos(shift * wave)
    sn_v[...] = jnp.sin(shift * wave)
    p_index = lax.broadcasted_iota(jnp.int32, (MODES, WAVES), 0).astype(F32)
    k_index = lax.broadcasted_iota(jnp.int32, (MODES, WAVES), 1).astype(F32)
    radial = (k_index / WAVES) ** 2 + (p_index / MODES) ** 2
    weight = (
        jnp.where(p_index == 0, 1.0, 2.0) / lat_count * (jnp.where(k_index == 0, 1.0, 2.0) / lon_count)
    )

    def rotation(f):
        damping = jnp.exp(-visc_ref[f // 4, f % 4] * radial) * weight
        return cs_v[pl.ds(f, 1), :] * damping, sn_v[pl.ds(f, 1), :] * damping

    lf = (lfh_ref, lfl_ref)
    lt = (lth_ref, ltl_ref)
    la = (lah_ref, lal_ref)
    at = (ath_ref, atl_ref)

    def both(pair):
        return pair[0][...], pair[1][...]

    load_state.wait()
    for copy in given[:6]:
        copy.wait()

    def forward(f, _):
        partial = halves(dot3(halves(state_v[f]), both(lf)))
        spectrum = dot3(both(at), partial)
        cosine, sine = rotation(f)
        a, b = spectrum[:, :WAVES], spectrum[:, WAVES:]
        rotated = jnp.concatenate([a * cosine - b * sine, a * sine + b * cosine], axis=1)
        put_rows(h32, pl.ds(f, lat_count, stride=fields), dot3(both(la), halves(rotated)))
        return 0

    lax.fori_loop(0, fields, forward, 0)

    def pack_rows(b, _):
        for r in range(2):
            rows = pl.ds(pl.multiple_of(b * 512, 512) + 256 * r, 256)
            packed = get_rows(h32, rows, 0, wave_tiles).astype(BF16)
            h16[b, :, pl.ds(16 * r, 16), :] = packed.reshape(levels, 16, waves)
        send_level(lambda to: h16.at[b, pl.ds(to, 1)], rh.at[b, mine], h_send, h_recv.at[b])
        rh[b, mine] = h16[b, mine]
        return 0

    lax.fori_loop(0, half // 2, pack_rows, 0)

    def later(b, _):
        deal_grad(2 * b, 0)
        deal_grad(2 * b + 1, 0)
        return pack_rows(b, 0)

    lax.fori_loop(half // 2, half, later, 0)

    for copy in given[6:]:
        copy.wait()

    order = order_ref[...]

    def units_first(bias_ref):
        bias = jnp.broadcast_to(bias_ref[...].reshape(1, hidden), (128, hidden)).T
        high, rest = halves(bias)
        mid, low = halves(bias - high.astype(F32))
        return dot(order, high) + dot(order, mid) + dot(order, low)

    win_t[...] = dot_nt(order, w_in_v[...]).astype(BF16)
    w_in_ref[...] = dot_nt(w_in_v[...], order).astype(BF16)
    w_mid_ref[...] = dot_nt(dot(order, w_mid_v[...]).astype(BF16), order).astype(BF16)
    wmid_t[...] = dot_nt(dot_nt(order, w_mid_v[...]).astype(BF16), order).astype(BF16)
    w_out = dot(order, w_out_v[...])
    w_out_ref[...] = w_out.astype(BF16)
    wout_t[...] = w_out.T.astype(BF16)
    bb1[...] = units_first(b_in_ref)
    bb2[...] = units_first(b_mid_ref)
    gi_a[...] = jnp.zeros_like(gi_a)
    gm_a[...] = jnp.zeros_like(gm_a)
    go_a[...] = jnp.zeros_like(go_a)
    s1_a[...] = jnp.zeros_like(s1_a)
    s2_a[...] = jnp.zeros_like(s2_a)

    def local(f, _):
        rows = get_rows(h32, pl.ds(f, lat_count, stride=fields), 0, wave_tiles)
        next_v[f] = dot3(halves(rows), both(lt))
        cot = cot_v[f]
        z_v[f] = dot(cot, lfh_ref[...]) + dot(cot, lfl_ref[...])
        return 0

    others = pl.ds(0, levels - 1)

    def wait_for(ref, sem):
        pltpu.make_async_copy(ref, ref, sem).wait()


    def lanes(x):
        x = x.reshape(levels, 2, 8, lon_count)
        return jnp.concatenate(
            [x[:, r].reshape(levels * 8, lon_count) for r in range(2)], axis=1
        ).astype(BF16)

    def rows_of(x0, x1, width):
        parts = [x.reshape(levels, 8, width) for x in (x0, x1)]
        return jnp.concatenate(parts, axis=1).astype(BF16)

    def lane_sum(x):
        out = x[:, :128]
        for c in range(1, x.shape[1] // 128):
            out = out + x[:, c * 128 : (c + 1) * 128]
        return out

    cols = 2 * lon_count

    def columns(a, _):
        wait_for(rg.at[a, others], g_recv.at[a])

        @pl.when(lax.rem(a, 2) == 0)
        def _():
            wait_for(rh.at[a // 2, others], h_recv.at[a // 2])

        in_pair = pl.ds(pl.multiple_of(16 * lax.rem(a, 2), 16), 16)
        spec = rh[a // 2, :, in_pair, :].reshape(levels * 16, waves)
        inp = lanes(dot(spec, lth_ref[...]) + dot(spec, ltl_ref[...]))
        gt = lanes(rg[a].reshape(levels * 16, lon_count).astype(F32))
        pre = dot(win_t[...], inp) + jnp.tile(bb1[...], (1, cols // 128))
        sg = sigmoid(pre)
        act = pre * sg
        slope1 = sg + act * (1.0 - sg)
        act1 = act.astype(BF16)
        pre = dot(wmid_t[...], act1) + jnp.tile(bb2[...], (1, cols // 128))
        sg = sigmoid(pre)
        act = pre * sg
        slope2 = sg + act * (1.0 - sg)
        act2 = act.astype(BF16)
        tend = dot(wout_t[...], act2)
        tb[a] = rows_of(tend[:, :lon_count], tend[:, lon_count:], lon_count)
        go_a[...] += dot_nt(act2, gt)
        slope = dot(w_out_ref[...], gt) * slope2
        s2_a[...] += lane_sum(slope)
        s2 = slope.astype(BF16)
        gm_a[...] += dot_nt(s2, act1)
        slope = dot(w_mid_ref[...], s2) * slope1
        s1_a[...] += lane_sum(slope)
        s1 = slope.astype(BF16)
        gi_a[...] += dot_nt(s1, inp)
        back = dot(w_in_ref[...], s1).astype(BF16)
        back = jnp.concatenate([back[:, :lon_count], back[:, lon_count:]], axis=0)
        back = dot(back, lfh_ref[...]) + dot(back, lfl_ref[...])
        half = levels * 8
        bb[a // 2, :, in_pair, :] = rows_of(back[:half], back[half:], waves)

        @pl.when(lax.rem(a, 2) == 1)
        def _():
            b = a // 2
            send_level(lambda to: bb.at[b, pl.ds(to, 1)], bbr.at[b, mine], b_send, b_recv)
            bbr[b, mine] = bb[b, mine]

        @pl.when(a < EARLY)
        def _():
            send_tend(a, 0)

        return 0

    def send_tend(a, _):
        send_level(lambda to: tb.at[a, pl.ds(to, 1)], tbr.at[a, mine], t_send, t_recv.at[a])
        tbr[a, mine] = tb[a, mine]
        return 0

    lax.fori_loop(0, blocks, columns, 0)
    lax.fori_loop(EARLY, EARLY + 2, send_tend, 0)

    lane = lax.broadcasted_iota(jnp.int32, (hidden, 128), 1)
    bias = jnp.where(lane == 0, jnp.sum(s1_a[...], axis=1, keepdims=True), 0.0)
    bias = jnp.where(lane == 1, jnp.sum(s2_a[...], axis=1, keepdims=True), bias)
    parts = [gi_a[...].astype(BF16), dot(gm_a[...].astype(BF16), order).astype(BF16)]
    parts += [go_a[...].astype(BF16), bias.astype(BF16)]
    gs[...] = jnp.concatenate(parts, axis=1).reshape(columns_x, hidden // columns_x, 768)
    for d, to in enumerate(beside):
        pltpu.make_async_remote_copy(
            gs.at[lax.rem(my_x + d + 1, columns_x)], gx.at[my_x], x_send, x_recv,
            device_id={"member": to}, device_id_type=MESH,
        ).start()
    gx[my_x] = gs[my_x]
    lax.fori_loop(0, fields, local, 0)

    wait_for(gx.at[pl.ds(0, columns_x - 1)], x_recv)
    total = gx[0].astype(F32)
    for s in range(1, columns_x):
        total = total + gx[s].astype(F32)
    total = total.astype(BF16)
    share = hidden // columns_x // levels
    place = lax.broadcasted_iota(jnp.int32, (levels * 8, hidden // columns_x), 0)
    unit = lax.broadcasted_iota(jnp.int32, (levels * 8, hidden // columns_x), 1)
    within = place & 7
    spread = jnp.where((unit == (place >> 3) * share + within) & (within < share), 1.0, 0.0).astype(BF16)
    pair = [dot(spread, total[:, c : c + 384]).reshape(levels, 8, 384) for c in (0, 384)]
    gl[...] = jnp.concatenate(pair, axis=1).astype(BF16)
    send_level(lambda to: gl.at[pl.ds(to, 1)], gr.at[mine], s_send, s_recv)
    gr[mine] = gl[mine]

    lax.fori_loop(EARLY + 2, blocks - 1, send_tend, 0)

    wait_for(bbr.at[:, others], b_recv)

    def gather(a, _):
        in_pair = pl.ds(pl.multiple_of(16 * lax.rem(a, 2), 16), 16)
        put_rows(b_v, slice(None), bbr[a // 2, :, in_pair, :].astype(F32).reshape(256, waves))
        rows = pl.ds(pl.multiple_of(a * 32, 32), 32)
        for f in range(fields):
            z_v[f, rows, :] += get_rows(b_v, pl.ds(f, 32, stride=fields), 0, wave_tiles)
        return 0

    lax.fori_loop(0, blocks, gather, 0)

    def backward(f, _):
        spectrum = dot3(both(at), halves(z_v[f]))
        cosine, sine = rotation(f)
        a, b = spectrum[:, :WAVES], spectrum[:, WAVES:]
        turned = jnp.concatenate([a * cosine + b * sine, b * cosine - a * sine], axis=1)
        rows = halves(dot3(both(la), halves(turned)))
        grad_v[f] = dot3(rows, both(lt))
        return 0

    lax.fori_loop(0, fields, backward, 0)

    def arrive(a, _):
        wait_for(tbr.at[a, others], t_recv.at[a])
        put_rows(t_v, slice(None), tbr[a].astype(F32).reshape(256, lon_count))
        rows = pl.ds(pl.multiple_of(a * 32, 32), 32)
        for f in range(fields):
            factor = 1.0 + noise_scale(f) * noise_v[f, rows, :].astype(F32)
            next_v[f, rows, :] += get_rows(t_v, pl.ds(f, 32, stride=fields), 0, lon_tiles) * factor
        return 0

    lax.fori_loop(0, half, arrive, 0)

    wait_for(gr.at[others], s_recv)
    total = gr[0].astype(F32)
    for s in range(1, levels):
        total = total + gr[s].astype(F32)
    ms[...] = total.astype(BF16)
    swap = pltpu.make_async_remote_copy(
        ms, mr, m_send, m_recv, device_id={"member": across}, device_id_type=MESH
    )
    swap.start()

    send_tend(blocks - 1, 0)
    lax.fori_loop(half, blocks, arrive, 0)

    swap.wait()
    norm = 1.0 / math.sqrt(members * lat_count * lon_count)
    sums_ref[...] = (total + mr[...].astype(F32)) * norm

    wait_for(g16.at[:, others], g_send)
    wait_for(h16.at[:, others], h_send)
    wait_for(tb.at[:, others], t_send)
    wait_for(bb.at[:, others], b_send)
    wait_for(gs.at[pl.ds(0, columns_x - 1)], x_send)
    wait_for(gl.at[others], s_send)


def finish(
    hidden, levels, members, next_in, grad_in, sums_ref, next_out, grad_out, gin_ref, gmid_ref,
    gout_ref, gbias_ref, sem,
):
    stores = []
    for i, (src, dst) in enumerate(((next_in, next_out), (grad_in, grad_out))):
        for f in range(src.shape[0]):
            stores.append(pltpu.make_async_copy(src.at[f], dst.at[f], sem.at[i, f]))
    for store in stores:
        store.start()
    own = hidden // levels // members
    first = lax.axis_index("member") // (members // 2) * own
    slot = lax.broadcasted_iota(jnp.int32, (8, 8), 0)
    unit = lax.broadcasted_iota(jnp.int32, (8, 8), 1)
    choose = jnp.where((unit == first + slot) & (slot < own), 1.0, 0.0)

    def exact(a, b, dims):
        return lax.dot_general(
            a, b, (dims, ((), ())), precision=lax.Precision.HIGHEST, preferred_element_type=F32
        )

    top = exact(choose, sums_ref[:8, :], ((1,), (0,)))
    low = exact(choose, sums_ref[8:, :], ((1,), (0,)))
    gin_ref[...] = top[:own, :128]
    gmid_ref[...] = jnp.concatenate([top[:, 128:], low[:, :128]], axis=1)[:own]
    gout_ref[...] = low[:own, 128:256]
    lane = lax.broadcasted_iota(jnp.int32, (8, 128), 1)
    row = lax.broadcasted_iota(jnp.int32, (8, 128), 0)
    take = jnp.where((lane == row) & (row < 2), 1.0, 0.0)
    gbias_ref[...] = exact(take, low[:, 256:], ((1,), (1,)))[:2, :own]
    for store in stores:
        store.wait()


def per_device(levels, members, state, noise, cot, shift, visc, ns, w_in, b_in, w_mid, b_mid, w_out):
    shape = state.shape
    lat_count, lon_count = shape[3:]
    fields = shape[0] * shape[1] * shape[2]
    hidden = w_in.shape[1]
    blocks = lat_count // 32
    waves = 2 * WAVES
    flat = (fields, lat_count, lon_count)
    own = hidden // levels // members
    smem = pl.BlockSpec(memory_space=pltpu.SMEM)
    hbm = pl.BlockSpec(memory_space=pl.ANY)
    vmem = pl.BlockSpec(memory_space=pltpu.VMEM)
    dma = pltpu.SemaphoreType.DMA
    given = [w_in, w_mid, w_out, *[jnp.asarray(t) for t in tables(lat_count, lon_count)]]
    given += [jnp.asarray(unit_order(hidden, levels, members)), b_in, b_mid]
    grid_rows = pltpu.VMEM((blocks, levels, 16, lon_count), BF16)
    wave_rows = pltpu.VMEM((blocks // 2, levels, 32, waves), BF16)
    per_unit = pltpu.VMEM((hidden, 128), F32)
    state_out, grad_out, sums = pl.pallas_call(
        functools.partial(kernel, levels, members, lat_count, lon_count, hidden),
        name="ensemble_step",
        out_shape=(
            pltpu.VMEM(flat, F32),
            pltpu.VMEM(flat, F32),
            pltpu.VMEM((16, 384), F32),
        ),
        in_specs=[smem] * 3 + [hbm] * (3 + len(given)),
        out_specs=(vmem, vmem, vmem),
        scratch_shapes=[pltpu.VMEM(x.shape, x.dtype) for x in given]
        + [pltpu.VMEM(x.shape, BF16) for x in given[:3]]
        + [
            pltpu.VMEM(flat, F32),
            pltpu.VMEM(flat, BF16),
            pltpu.VMEM(flat, BF16),
            grid_rows, grid_rows, wave_rows, wave_rows, grid_rows, grid_rows, wave_rows, wave_rows,
            pltpu.VMEM((fields, lat_count, waves), F32),
            pltpu.VMEM((waves // 128, lat_count * fields, 128), F32),
            pltpu.VMEM((lon_count // 128, 256, 128), F32),
            pltpu.VMEM((lon_count // 128, 256, 128), F32),
            pltpu.VMEM((waves // 128, 256, 128), F32),
            pltpu.VMEM((hidden, w_in.shape[0]), BF16),
            pltpu.VMEM((hidden, hidden), BF16),
            pltpu.VMEM((w_out.shape[1], hidden), BF16),
            per_unit, per_unit,
            pltpu.VMEM((fields, WAVES), F32),
            pltpu.VMEM((fields, WAVES), F32),
            per_unit,
            pltpu.VMEM((hidden, hidden), F32),
            per_unit, per_unit, per_unit,
            pltpu.VMEM((members // 2, hidden // (members // 2), 768), BF16),
            pltpu.VMEM((members // 2, hidden // (members // 2), 768), BF16),
            pltpu.VMEM((levels, 16, 384), BF16),
            pltpu.VMEM((levels, 16, 384), BF16),
            pltpu.VMEM((16, 384), BF16),
            pltpu.VMEM((16, 384), BF16),
            dma((2, blocks)), dma(()), dma((len(given),)),
            dma(()), dma((blocks,)), dma(()), dma((blocks // 2,)), dma(()), dma((blocks,)),
            dma(()), dma(()), dma(()), dma(()), dma(()), dma(()), dma(()), dma(()),
        ],
        compiler_params=pltpu.CompilerParams(
            collective_id=0, has_side_effects=True, vmem_limit_bytes=VMEM_LIMIT
        ),
    )(
        shift, visc, ns,
        *[pltpu.with_memory_space_constraint(x, pltpu.HBM)
          for x in (state.reshape(flat), noise.reshape(flat), cot.reshape(flat), *given)],
    )
    out = pl.pallas_call(
        functools.partial(finish, hidden, levels, members),
        name="finish",
        out_shape=(
            jax.ShapeDtypeStruct(flat, F32),
            jax.ShapeDtypeStruct(flat, F32),
            jax.ShapeDtypeStruct((own, w_in.shape[0]), F32),
            jax.ShapeDtypeStruct((own, hidden), F32),
            jax.ShapeDtypeStruct((own, w_out.shape[1]), F32),
            jax.ShapeDtypeStruct((2, own), F32),
        ),
        in_specs=[vmem, vmem, vmem],
        out_specs=(hbm, hbm, vmem, vmem, vmem, vmem),
        scratch_shapes=[dma((2, fields))],
        compiler_params=pltpu.CompilerParams(vmem_limit_bytes=32 << 20),
    )(state_out, grad_out, sums)
    return (
        out[0].reshape(shape), out[1].reshape(shape), out[2].T, out[3].T, out[4].T, out[5],
    )


def solution(mesh):
    grid = P("member", "level", None, None, None)
    return jax.shard_map(
        functools.partial(per_device, mesh.shape["level"], mesh.shape["member"]),
        mesh=mesh,
        in_specs=(grid, grid, grid, P("level", None), P("level", None), P("level", None))
        + (P(),) * 5,
        out_specs=(grid, grid) + (P(None, ("level", "member")),) * 4,
        check_vma=False,
    )
```

```python
import functools
import math

import jax
import jax.numpy as jnp
import ml_dtypes
import numpy as np
from jax import lax
from jax.experimental import pallas as pl
from jax.experimental.pallas import tpu as pltpu
from jax.sharding import PartitionSpec as P

WAVES = 128
MODES = 128
F32 = jnp.float32
BF16 = jnp.bfloat16
MESH = pl.DeviceIdType.MESH
EARLY = 1
STRIDE = 7
VMEM_LIMIT = 46 << 20


def halves_np(table):
    high = table.astype(ml_dtypes.bfloat16)
    low = (table - high.astype(np.float64)).astype(ml_dtypes.bfloat16)
    return high, low


def tables(lat_count, lon_count):
    lon = np.arange(lon_count)[:, None] * np.arange(WAVES)[None, :] % lon_count
    phase = 2.0 * np.pi * lon / lon_count
    lon_fwd = np.concatenate([np.cos(phase), np.sin(phase)], axis=1)
    turn = (2 * np.arange(lat_count)[:, None] + 1) * np.arange(MODES)[None, :] % (4 * lat_count)
    lat_fwd = np.cos(np.pi * turn / (2 * lat_count))
    out = []
    for table in (lon_fwd, lon_fwd.T, lat_fwd, lat_fwd.T):
        out.extend(halves_np(np.ascontiguousarray(table)))
    return out


def unit_order(hidden, levels, members):
    columns = members // 2
    units = np.arange(hidden).reshape(levels, 2, columns, -1)
    order = units.transpose(2, 0, 1, 3).reshape(-1)
    return (order[:, None] == np.arange(hidden)[None, :]).astype(ml_dtypes.bfloat16)


def halves(x):
    high = x.astype(BF16)
    return high, (x - high.astype(F32)).astype(BF16)


def dot(a, b):
    return jnp.dot(a, b, preferred_element_type=F32)


def dot_nt(a, b):
    return lax.dot_general(a, b, (((1,), (1,)), ((), ())), preferred_element_type=F32)


def dot3(a, b):
    return dot(a[0], b[0]) + dot(a[0], b[1]) + dot(a[1], b[0])


def put_rows(ref, rows, x):
    for c in range(x.shape[1] // 128):
        ref[c, rows, :] = x[:, c * 128 : (c + 1) * 128]


def get_rows(ref, rows, first, count):
    return jnp.concatenate([ref[c, rows, :] for c in range(first, first + count)], axis=1)


def sigmoid(x):
    return 0.5 * jnp.tanh(0.5 * x) + 0.5


def kernel(
    levels, members, lat_count, lon_count, hidden,
    shift_ref, visc_ref, ns_ref, state_hbm, noise_hbm, cot_hbm,
    w_in_hbm, w_mid_hbm, w_out_hbm, lfh_hbm, lfl_hbm, lth_hbm, ltl_hbm, lah_hbm, lal_hbm, ath_hbm, atl_hbm,
    order_hbm, b_in_hbm, b_mid_hbm,
    next_v, grad_v, sums_ref,
    w_in_v, w_mid_v, w_out_v, lfh_ref, lfl_ref, lth_ref, ltl_ref, lah_ref, lal_ref, ath_ref, atl_ref,
    order_ref, b_in_ref, b_mid_ref,
    w_in_ref, w_mid_ref, w_out_ref,
    state_v, noise_v, cot_v, g16, rg, h16, rh, tb, tbr, bb, bbr, z_v, h32, st_v, t_v, b_v,
    win_t, wmid_t, wout_t, bb1, bb2, cs_v, sn_v, gi_a, gm_a, go_a, s1_a, s2_a,
    gs, gx, gl, gr, ms, mr,
    in_sem, state_sem, w_sem, g_send, g_recv, h_send, h_recv, t_send, t_recv, b_send, b_recv,
    x_send, x_recv, s_send, s_recv, m_send, m_recv,
):
    me = lax.axis_index("level")
    mem = lax.axis_index("member")
    blocks = lat_count // 32
    fields = 8
    waves = 2 * WAVES
    lon_tiles = lon_count // 128
    wave_tiles = waves // 128

    def load_block(a):
        rows = pl.ds(pl.multiple_of(a * 32, 32), 32)
        return (
            pltpu.make_async_copy(noise_hbm.at[:, rows], noise_v.at[:, rows], in_sem.at[0, a]),
            pltpu.make_async_copy(cot_hbm.at[:, rows], cot_v.at[:, rows], in_sem.at[1, a]),
        )

    for copy in load_block(0):
        copy.start()

    barrier = pltpu.get_barrier_semaphore()

    def greet_level(d, _):
        pl.semaphore_signal(
            barrier, inc=1, device_id={"level": lax.rem(me + d, levels)}, device_id_type=MESH
        )
        return 0

    columns_x = members // 2
    my_y, my_x = mem // columns_x, lax.rem(mem, columns_x)
    beside = [my_y * columns_x + lax.rem(my_x + d, columns_x) for d in range(1, columns_x)]
    across = (1 - my_y) * columns_x + my_x

    for to in (*beside, across):
        pl.semaphore_signal(barrier, inc=1, device_id={"member": to}, device_id_type=MESH)
    lax.fori_loop(1, levels, greet_level, 0)

    for a in range(1, blocks):
        for copy in load_block(a):
            copy.start()
    load_state = pltpu.make_async_copy(state_hbm, state_v, state_sem)
    load_state.start()
    given = [
        pltpu.make_async_copy(src, dst, w_sem.at[i])
        for i, (src, dst) in enumerate(
            [
                (lfh_hbm, lfh_ref), (lfl_hbm, lfl_ref), (ath_hbm, ath_ref), (atl_hbm, atl_ref),
                (lah_hbm, lah_ref), (lal_hbm, lal_ref), (lth_hbm, lth_ref), (ltl_hbm, ltl_ref),
                (w_in_hbm, w_in_v), (w_mid_hbm, w_mid_v), (w_out_hbm, w_out_v), (order_hbm, order_ref),
                (b_in_hbm, b_in_ref), (b_mid_hbm, b_mid_ref),
            ]
        )
    ]
    for copy in given:
        copy.start()

    def send_level(src, dst, send, recv):
        def one(d, _):
            to = lax.rem(me + STRIDE * d, levels)
            pltpu.make_async_remote_copy(
                src(to), dst, send, recv, device_id={"level": to}, device_id_type=MESH
            ).start()
            return 0

        lax.fori_loop(1, levels, one, 0)

    mine = pl.ds(me, 1)

    def noise_scale(f):
        return ns_ref[f // 4, f % 4]

    def make_grad(a, _):
        for copy in load_block(a):
            copy.wait()
        rows = pl.ds(pl.multiple_of(a * 32, 32), 32)
        for f in range(fields):
            factor = 1.0 + noise_scale(f) * noise_v[f, rows, :].astype(F32)
            put_rows(st_v, pl.ds(f, 32, stride=fields), cot_v[f, rows, :].astype(F32) * factor)
        g16[a] = get_rows(st_v, slice(None), 0, lon_tiles).astype(BF16).reshape(levels, 16, lon_count)
        return 0

    def send_grad(a, _):
        send_level(lambda to: g16.at[a, pl.ds(to, 1)], rg.at[a, mine], g_send, g_recv.at[a])
        rg[a, mine] = g16[a, mine]
        return 0

    def deal_grad(a, _):
        make_grad(a, 0)
        return send_grad(a, 0)

    half = blocks // 2
    make_grad(0, 0)
    pl.semaphore_wait(barrier, levels - 1 + columns_x)
    send_grad(0, 0)
    lax.fori_loop(1, half, deal_grad, 0)

    field_row = lax.broadcasted_iota(jnp.int32, (fields, WAVES), 0)
    wave = lax.broadcasted_iota(jnp.int32, (fields, WAVES), 1).astype(F32)
    shift = jnp.zeros((fields, WAVES), F32)
    for f in range(fields):
        shift = jnp.where(field_row == f, shift_ref[f // 4, f % 4], shift)
    cs_v[...] = jnp.cos(shift * wave)
    sn_v[...] = jnp.sin(shift * wave)
    p_index = lax.broadcasted_iota(jnp.int32, (MODES, WAVES), 0).astype(F32)
    k_index = lax.broadcasted_iota(jnp.int32, (MODES, WAVES), 1).astype(F32)
    radial = (k_index / WAVES) ** 2 + (p_index / MODES) ** 2
    weight = (
        jnp.where(p_index == 0, 1.0, 2.0) / lat_count * (jnp.where(k_index == 0, 1.0, 2.0) / lon_count)
    )

    def rotation(f):
        damping = jnp.exp(-visc_ref[f // 4, f % 4] * radial) * weight
        return cs_v[pl.ds(f, 1), :] * damping, sn_v[pl.ds(f, 1), :] * damping

    lf = (lfh_ref, lfl_ref)
    lt = (lth_ref, ltl_ref)
    la = (lah_ref, lal_ref)
    at = (ath_ref, atl_ref)

    def both(pair):
        return pair[0][...], pair[1][...]

    load_state.wait()
    for copy in given[:6]:
        copy.wait()

    def forward(f, _):
        partial = halves(dot3(halves(state_v[f]), both(lf)))
        spectrum = dot3(both(at), partial)
        cosine, sine = rotation(f)
        a, b = spectrum[:, :WAVES], spectrum[:, WAVES:]
        rotated = jnp.concatenate([a * cosine - b * sine, a * sine + b * cosine], axis=1)
        put_rows(h32, pl.ds(f, lat_count, stride=fields), dot3(both(la), halves(rotated)))
        return 0

    lax.fori_loop(0, fields, forward, 0)

    def pack_rows(b, _):
        for r in range(2):
            rows = pl.ds(pl.multiple_of(b * 512, 512) + 256 * r, 256)
            packed = get_rows(h32, rows, 0, wave_tiles).astype(BF16)
            h16[b, :, pl.ds(16 * r, 16), :] = packed.reshape(levels, 16, waves)
        send_level(lambda to: h16.at[b, pl.ds(to, 1)], rh.at[b, mine], h_send, h_recv.at[b])
        rh[b, mine] = h16[b, mine]
        return 0

    lax.fori_loop(0, half // 2, pack_rows, 0)

    def later(b, _):
        deal_grad(2 * b, 0)
        deal_grad(2 * b + 1, 0)
        return pack_rows(b, 0)

    lax.fori_loop(half // 2, half, later, 0)

    for copy in given[6:]:
        copy.wait()

    order = order_ref[...]

    def units_first(bias_ref):
        bias = jnp.broadcast_to(bias_ref[...].reshape(1, hidden), (128, hidden)).T
        high, rest = halves(bias)
        mid, low = halves(bias - high.astype(F32))
        return dot(order, high) + dot(order, mid) + dot(order, low)

    win_t[...] = dot_nt(order, w_in_v[...]).astype(BF16)
    w_in_ref[...] = dot_nt(w_in_v[...], order).astype(BF16)
    w_mid_ref[...] = dot_nt(dot(order, w_mid_v[...]).astype(BF16), order).astype(BF16)
    wmid_t[...] = dot_nt(dot_nt(order, w_mid_v[...]).astype(BF16), order).astype(BF16)
    w_out = dot(order, w_out_v[...])
    w_out_ref[...] = w_out.astype(BF16)
    wout_t[...] = w_out.T.astype(BF16)
    bb1[...] = units_first(b_in_ref)
    bb2[...] = units_first(b_mid_ref)
    gi_a[...] = jnp.zeros_like(gi_a)
    gm_a[...] = jnp.zeros_like(gm_a)
    go_a[...] = jnp.zeros_like(go_a)
    s1_a[...] = jnp.zeros_like(s1_a)
    s2_a[...] = jnp.zeros_like(s2_a)

    def local(f, _):
        rows = get_rows(h32, pl.ds(f, lat_count, stride=fields), 0, wave_tiles)
        next_v[f] = dot3(halves(rows), both(lt))
        cot = cot_v[f]
        z_v[f] = dot(cot, lfh_ref[...]) + dot(cot, lfl_ref[...])
        return 0

    others = pl.ds(0, levels - 1)

    def wait_for(ref, sem):
        pltpu.make_async_copy(ref, ref, sem).wait()


    def lanes(x):
        x = x.reshape(levels, 2, 8, lon_count)
        return jnp.concatenate(
            [x[:, r].reshape(levels * 8, lon_count) for r in range(2)], axis=1
        ).astype(BF16)

    def rows_of(x0, x1, width):
        parts = [x.reshape(levels, 8, width) for x in (x0, x1)]
        return jnp.concatenate(parts, axis=1).astype(BF16)

    def lane_sum(x):
        out = x[:, :128]
        for c in range(1, x.shape[1] // 128):
            out = out + x[:, c * 128 : (c + 1) * 128]
        return out

    cols = 2 * lon_count

    def columns(a, _):
        wait_for(rg.at[a, others], g_recv.at[a])

        @pl.when(lax.rem(a, 2) == 0)
        def _():
            wait_for(rh.at[a // 2, others], h_recv.at[a // 2])

        in_pair = pl.ds(pl.multiple_of(16 * lax.rem(a, 2), 16), 16)
        spec = rh[a // 2, :, in_pair, :].reshape(levels * 16, waves)
        inp = lanes(dot(spec, lth_ref[...]) + dot(spec, ltl_ref[...]))
        gt = lanes(rg[a].reshape(levels * 16, lon_count).astype(F32))
        pre = dot(win_t[...], inp) + jnp.tile(bb1[...], (1, cols // 128))
        sg = sigmoid(pre)
        act = pre * sg
        slope1 = sg + act * (1.0 - sg)
        act1 = act.astype(BF16)
        pre = dot(wmid_t[...], act1) + jnp.tile(bb2[...], (1, cols // 128))
        sg = sigmoid(pre)
        act = pre * sg
        slope2 = sg + act * (1.0 - sg)
        act2 = act.astype(BF16)
        tend = dot(wout_t[...], act2)
        tb[a] = rows_of(tend[:, :lon_count], tend[:, lon_count:], lon_count)
        go_a[...] += dot_nt(act2, gt)
        slope = dot(w_out_ref[...], gt) * slope2
        s2_a[...] += lane_sum(slope)
        s2 = slope.astype(BF16)
        gm_a[...] += dot_nt(s2, act1)
        slope = dot(w_mid_ref[...], s2) * slope1
        s1_a[...] += lane_sum(slope)
        s1 = slope.astype(BF16)
        gi_a[...] += dot_nt(s1, inp)
        back = dot(w_in_ref[...], s1).astype(BF16)
        back = jnp.concatenate([back[:, :lon_count], back[:, lon_count:]], axis=0)
        back = dot(back, lfh_ref[...]) + dot(back, lfl_ref[...])
        half = levels * 8
        bb[a // 2, :, in_pair, :] = rows_of(back[:half], back[half:], waves)

        @pl.when(lax.rem(a, 2) == 1)
        def _():
            b = a // 2
            send_level(lambda to: bb.at[b, pl.ds(to, 1)], bbr.at[b, mine], b_send, b_recv)
            bbr[b, mine] = bb[b, mine]

        @pl.when(a < EARLY)
        def _():
            send_tend(a, 0)

        return 0

    def send_tend(a, _):
        send_level(lambda to: tb.at[a, pl.ds(to, 1)], tbr.at[a, mine], t_send, t_recv.at[a])
        tbr[a, mine] = tb[a, mine]
        return 0

    lax.fori_loop(0, blocks, columns, 0)
    lax.fori_loop(EARLY, EARLY + 2, send_tend, 0)

    lane = lax.broadcasted_iota(jnp.int32, (hidden, 128), 1)
    bias = jnp.where(lane == 0, jnp.sum(s1_a[...], axis=1, keepdims=True), 0.0)
    bias = jnp.where(lane == 1, jnp.sum(s2_a[...], axis=1, keepdims=True), bias)
    parts = [gi_a[...].astype(BF16), dot(gm_a[...].astype(BF16), order).astype(BF16)]
    parts += [go_a[...].astype(BF16), bias.astype(BF16)]
    gs[...] = jnp.concatenate(parts, axis=1).reshape(columns_x, hidden // columns_x, 768)
    for d, to in enumerate(beside):
        pltpu.make_async_remote_copy(
            gs.at[lax.rem(my_x + d + 1, columns_x)], gx.at[my_x], x_send, x_recv,
            device_id={"member": to}, device_id_type=MESH,
        ).start()
    gx[my_x] = gs[my_x]
    lax.fori_loop(0, fields, local, 0)

    wait_for(gx.at[pl.ds(0, columns_x - 1)], x_recv)
    total = gx[0].astype(F32)
    for s in range(1, columns_x):
        total = total + gx[s].astype(F32)
    total = total.astype(BF16)
    share = hidden // columns_x // levels
    place = lax.broadcasted_iota(jnp.int32, (levels * 8, hidden // columns_x), 0)
    unit = lax.broadcasted_iota(jnp.int32, (levels * 8, hidden // columns_x), 1)
    within = place & 7
    spread = jnp.where((unit == (place >> 3) * share + within) & (within < share), 1.0, 0.0).astype(BF16)
    pair = [dot(spread, total[:, c : c + 384]).reshape(levels, 8, 384) for c in (0, 384)]
    gl[...] = jnp.concatenate(pair, axis=1).astype(BF16)
    send_level(lambda to: gl.at[pl.ds(to, 1)], gr.at[mine], s_send, s_recv)
    gr[mine] = gl[mine]

    lax.fori_loop(EARLY + 2, blocks - 1, send_tend, 0)

    wait_for(bbr.at[:, others], b_recv)

    def gather(a, _):
        in_pair = pl.ds(pl.multiple_of(16 * lax.rem(a, 2), 16), 16)
        put_rows(b_v, slice(None), bbr[a // 2, :, in_pair, :].astype(F32).reshape(256, waves))
        rows = pl.ds(pl.multiple_of(a * 32, 32), 32)
        for f in range(fields):
            z_v[f, rows, :] += get_rows(b_v, pl.ds(f, 32, stride=fields), 0, wave_tiles)
        return 0

    lax.fori_loop(0, blocks, gather, 0)

    def backward(f, _):
        spectrum = dot3(both(at), halves(z_v[f]))
        cosine, sine = rotation(f)
        a, b = spectrum[:, :WAVES], spectrum[:, WAVES:]
        turned = jnp.concatenate([a * cosine + b * sine, b * cosine - a * sine], axis=1)
        rows = halves(dot3(both(la), halves(turned)))
        grad_v[f] = dot3(rows, both(lt))
        return 0

    lax.fori_loop(0, fields, backward, 0)

    def arrive(a, _):
        wait_for(tbr.at[a, others], t_recv.at[a])
        put_rows(t_v, slice(None), tbr[a].astype(F32).reshape(256, lon_count))
        rows = pl.ds(pl.multiple_of(a * 32, 32), 32)
        for f in range(fields):
            factor = 1.0 + noise_scale(f) * noise_v[f, rows, :].astype(F32)
            next_v[f, rows, :] += get_rows(t_v, pl.ds(f, 32, stride=fields), 0, lon_tiles) * factor
        return 0

    lax.fori_loop(0, half, arrive, 0)

    wait_for(gr.at[others], s_recv)
    total = gr[0].astype(F32)
    for s in range(1, levels):
        total = total + gr[s].astype(F32)
    ms[...] = total.astype(BF16)
    swap = pltpu.make_async_remote_copy(
        ms, mr, m_send, m_recv, device_id={"member": across}, device_id_type=MESH
    )
    swap.start()

    send_tend(blocks - 1, 0)
    lax.fori_loop(half, blocks, arrive, 0)

    swap.wait()
    norm = 1.0 / math.sqrt(members * lat_count * lon_count)
    sums_ref[...] = (total + mr[...].astype(F32)) * norm

    wait_for(g16.at[:, others], g_send)
    wait_for(h16.at[:, others], h_send)
    wait_for(tb.at[:, others], t_send)
    wait_for(bb.at[:, others], b_send)
    wait_for(gs.at[pl.ds(0, columns_x - 1)], x_send)
    wait_for(gl.at[others], s_send)


def finish(
    hidden, levels, members, next_in, grad_in, sums_ref, next_out, grad_out, gin_ref, gmid_ref,
    gout_ref, gbias_ref, sem,
):
    stores = []
    for i, (src, dst) in enumerate(((next_in, next_out), (grad_in, grad_out))):
        for f in range(src.shape[0]):
            stores.append(pltpu.make_async_copy(src.at[f], dst.at[f], sem.at[i, f]))
    for store in stores:
        store.start()
    own = hidden // levels // members
    first = lax.axis_index("member") // (members // 2) * own
    slot = lax.broadcasted_iota(jnp.int32, (8, 8), 0)
    unit = lax.broadcasted_iota(jnp.int32, (8, 8), 1)
    choose = jnp.where((unit == first + slot) & (slot < own), 1.0, 0.0)

    def exact(a, b, dims):
        return lax.dot_general(
            a, b, (dims, ((), ())), precision=lax.Precision.HIGHEST, preferred_element_type=F32
        )

    top = exact(choose, sums_ref[:8, :], ((1,), (0,)))
    low = exact(choose, sums_ref[8:, :], ((1,), (0,)))
    gin_ref[...] = top[:own, :128]
    gmid_ref[...] = jnp.concatenate([top[:, 128:], low[:, :128]], axis=1)[:own]
    gout_ref[...] = low[:own, 128:256]
    lane = lax.broadcasted_iota(jnp.int32, (8, 128), 1)
    row = lax.broadcasted_iota(jnp.int32, (8, 128), 0)
    take = jnp.where((lane == row) & (row < 2), 1.0, 0.0)
    gbias_ref[...] = exact(take, low[:, 256:], ((1,), (1,)))[:2, :own]
    for store in stores:
        store.wait()


def per_device(levels, members, state, noise, cot, shift, visc, ns, w_in, b_in, w_mid, b_mid, w_out):
    shape = state.shape
    lat_count, lon_count = shape[3:]
    fields = shape[0] * shape[1] * shape[2]
    hidden = w_in.shape[1]
    blocks = lat_count // 32
    waves = 2 * WAVES
    flat = (fields, lat_count, lon_count)
    own = hidden // levels // members
    smem = pl.BlockSpec(memory_space=pltpu.SMEM)
    hbm = pl.BlockSpec(memory_space=pl.ANY)
    vmem = pl.BlockSpec(memory_space=pltpu.VMEM)
    dma = pltpu.SemaphoreType.DMA
    given = [w_in, w_mid, w_out, *[jnp.asarray(t) for t in tables(lat_count, lon_count)]]
    given += [jnp.asarray(unit_order(hidden, levels, members)), b_in, b_mid]
    grid_rows = pltpu.VMEM((blocks, levels, 16, lon_count), BF16)
    wave_rows = pltpu.VMEM((blocks // 2, levels, 32, waves), BF16)
    per_unit = pltpu.VMEM((hidden, 128), F32)
    state_out, grad_out, sums = pl.pallas_call(
        functools.partial(kernel, levels, members, lat_count, lon_count, hidden),
        name="ensemble_step",
        out_shape=(
            pltpu.VMEM(flat, F32),
            pltpu.VMEM(flat, F32),
            pltpu.VMEM((16, 384), F32),
        ),
        in_specs=[smem] * 3 + [hbm] * (3 + len(given)),
        out_specs=(vmem, vmem, vmem),
        scratch_shapes=[pltpu.VMEM(x.shape, x.dtype) for x in given]
        + [pltpu.VMEM(x.shape, BF16) for x in given[:3]]
        + [
            pltpu.VMEM(flat, F32),
            pltpu.VMEM(flat, BF16),
            pltpu.VMEM(flat, BF16),
            grid_rows, grid_rows, wave_rows, wave_rows, grid_rows, grid_rows, wave_rows, wave_rows,
            pltpu.VMEM((fields, lat_count, waves), F32),
            pltpu.VMEM((waves // 128, lat_count * fields, 128), F32),
            pltpu.VMEM((lon_count // 128, 256, 128), F32),
            pltpu.VMEM((lon_count // 128, 256, 128), F32),
            pltpu.VMEM((waves // 128, 256, 128), F32),
            pltpu.VMEM((hidden, w_in.shape[0]), BF16),
            pltpu.VMEM((hidden, hidden), BF16),
            pltpu.VMEM((w_out.shape[1], hidden), BF16),
            per_unit, per_unit,
            pltpu.VMEM((fields, WAVES), F32),
            pltpu.VMEM((fields, WAVES), F32),
            per_unit,
            pltpu.VMEM((hidden, hidden), F32),
            per_unit, per_unit, per_unit,
            pltpu.VMEM((members // 2, hidden // (members // 2), 768), BF16),
            pltpu.VMEM((members // 2, hidden // (members // 2), 768), BF16),
            pltpu.VMEM((levels, 16, 384), BF16),
            pltpu.VMEM((levels, 16, 384), BF16),
            pltpu.VMEM((16, 384), BF16),
            pltpu.VMEM((16, 384), BF16),
            dma((2, blocks)), dma(()), dma((len(given),)),
            dma(()), dma((blocks,)), dma(()), dma((blocks // 2,)), dma(()), dma((blocks,)),
            dma(()), dma(()), dma(()), dma(()), dma(()), dma(()), dma(()), dma(()),
        ],
        compiler_params=pltpu.CompilerParams(
            collective_id=0, has_side_effects=True, vmem_limit_bytes=VMEM_LIMIT
        ),
    )(
        shift, visc, ns,
        *[pltpu.with_memory_space_constraint(x, pltpu.HBM)
          for x in (state.reshape(flat), noise.reshape(flat), cot.reshape(flat), *given)],
    )
    out = pl.pallas_call(
        functools.partial(finish, hidden, levels, members),
        name="finish",
        out_shape=(
            jax.ShapeDtypeStruct(flat, F32),
            jax.ShapeDtypeStruct(flat, F32),
            jax.ShapeDtypeStruct((own, w_in.shape[0]), F32),
            jax.ShapeDtypeStruct((own, hidden), F32),
            jax.ShapeDtypeStruct((own, w_out.shape[1]), F32),
            jax.ShapeDtypeStruct((2, own), F32),
        ),
        in_specs=[vmem, vmem, vmem],
        out_specs=(hbm, hbm, vmem, vmem, vmem, vmem),
        scratch_shapes=[dma((2, fields))],
        compiler_params=pltpu.CompilerParams(vmem_limit_bytes=32 << 20),
    )(state_out, grad_out, sums)
    return (
        out[0].reshape(shape), out[1].reshape(shape), out[2].T, out[3].T, out[4].T, out[5],
    )


def solution(mesh):
    grid = P("member", "level", None, None, None)
    return jax.shard_map(
        functools.partial(per_device, mesh.shape["level"], mesh.shape["member"]),
        mesh=mesh,
        in_specs=(grid, grid, grid, P("level", None), P("level", None), P("level", None))
        + (P(),) * 5,
        out_specs=(grid, grid) + (P(None, ("level", "member")),) * 4,
        check_vma=False,
    )
```
